512 devices in a mesh: src: 16 (over z, y_hi), tgt: 32 (over x, y_lo, core).
Axes of the slice: x: 4, y: 8 (y_hi: 2, y_lo: 4; y = y_hi * 4 + y_lo), z: 8, core: 2. Of those that a mesh axis runs over, the one named last changes fastest.
Arguments:
- coupling: bfloat16 [8192, 16384], P('src', 'tgt'), may hold values from 0.25 to 4
- src_pcs: bfloat16 [50, 8192], P(None, 'src'), may hold values from -24 to 24
- tgt_pcs: bfloat16 [50, 16384], P(None, 'tgt'), may hold values from -24 to 24
- src_mass: float32 [8192], P('src'), may hold values from 0.25 to 4
- tgt_mass: float32 [16384], P('tgt'), may hold values from 0.25 to 4
Outputs:
- log_coupling: float32 [8192, 16384], P('src', 'tgt')
- row_potential: float32 [8192], P('src')
- col_potential: float32 [16384], P('tgt')
The draws below stay inside these ranges and needn't reach their ends.
All inputs are finite; a program needn't handle non-finite values.
Results may differ from the reference program's by a relative error of at most 0.0019.
Values sent between devices are 32-bit elements; how exact they have to be, the bound alone decides.
A program may use at most 64 MiB of HBM per device.

```python
import math
import jax
import jax.numpy as jnp
from jax import lax

PCS = 50
ITERS = 4
NS = 8192
NT = 16384


def pc_field(key, cells):
    entry_key, scale_key = jax.random.split(key)
    leading = 2.0
    entries = jax.random.truncated_normal(entry_key, -4.0, 4.0, (PCS, cells), jnp.float32)
    components = leading * 0.1 ** (jnp.arange(PCS, dtype=jnp.float32) / (PCS - 1))
    cell_scale = jnp.exp(jax.random.uniform(scale_key, (cells,), jnp.float32, jnp.log(0.3), jnp.log(3.0)))
    return (entries * components[:, None] * cell_scale[None, :]).astype(jnp.bfloat16)


def draw_src_pcs(key, part):
    return pc_field(jax.random.fold_in(key, 11), NS)


def draw_tgt_pcs(key, part):
    return pc_field(jax.random.fold_in(key, 23), NT)


def block_levels(own_key, extent, cuts, smallest, high):
    def one(position, shards_of):
        heights = jax.random.uniform(jax.random.fold_in(jax.random.fold_in(own_key, 6), position), (shards_of,), jnp.float32, smallest / len(cuts), high / len(cuts))
        return jnp.repeat(jnp.exp(heights), extent[position] // shards_of).reshape((-1,) + (1,) * (len(extent) - position - 1))

    loudness = one(*cuts[0])
    for cut in cuts[1:]:
        loudness = loudness * one(*cut)
    return loudness


def setup_inputs(seed: int = 0) -> dict:
    splits = jax.random.split(jax.random.key(seed), 6)
    return {
        "coupling": jnp.clip(jnp.exp(math.log(4.0) - 2.7725887 * jax.random.uniform(splits[0], (NS, NT), jnp.float32) ** block_levels(splits[0], (NS, NT), ((0, 16), (1, 32)), -0.2, 0.2)), 0.25, 4.0).astype(jnp.bfloat16),
        "src_pcs": draw_src_pcs(jax.random.fold_in(splits[5], 71), 0),
        "tgt_pcs": draw_tgt_pcs(jax.random.fold_in(splits[5], 71), 0),
        "src_mass": jnp.clip(jnp.exp(math.log(4.0) - 2.7725887 * jax.random.uniform(splits[3], (NS,), jnp.float32) ** block_levels(splits[3], (NS,), ((0, 16),), -0.2, 0.2)), 0.25, 4.0),
        "tgt_mass": jnp.clip(jnp.exp(math.log(4.0) - 2.7725887 * jax.random.uniform(splits[4], (NT,), jnp.float32) ** block_levels(splits[4], (NT,), ((0, 32),), -0.2, 0.2)), 0.25, 4.0),
    }


eps_reg = 0.5
marg_power = 1.0 / (1.0 + eps_reg)
tiny_eps = 1e-06

def reference(coupling, src_pcs, tgt_pcs, src_mass, tgt_mass):
    exact = lax.Precision.HIGHEST
    panel = jnp.dot(src_pcs, coupling, preferred_element_type=jnp.float32)
    moment = jnp.dot(panel, tgt_pcs.astype(jnp.float32).T, precision=exact) * (NS * NT) ** (-0.5)
    normed = moment / jnp.sqrt(jnp.mean(moment * moment) + tiny_eps)
    weighted = jnp.dot(normed, tgt_pcs.astype(jnp.float32), precision=exact)
    scores = jnp.dot(src_pcs.astype(jnp.float32).T, weighted, precision=exact) * (2.0 / (eps_reg * PCS))
    log_src = jnp.log(src_mass)
    log_tgt = jnp.log(tgt_mass)
    col_potential = jnp.zeros((NT,), jnp.float32)
    row_potential = jnp.zeros((NS,), jnp.float32)
    for iteration in range(ITERS):
        shifted = scores + col_potential[None, :]
        highest = lax.optimization_barrier(jnp.max(shifted, axis=1))
        summed_exp = lax.optimization_barrier(jnp.sum(jnp.exp(shifted - highest[:, None]), axis=1))
        row_potential = marg_power * (log_src - (highest + jnp.log(summed_exp) - jnp.log(jnp.float32(NT))))
        shifted = scores + row_potential[:, None]
        highest = lax.optimization_barrier(jnp.max(shifted, axis=0))
        summed_exp = lax.optimization_barrier(jnp.sum(jnp.exp(shifted - highest[None, :]), axis=0))
        col_potential = marg_power * (log_tgt - (highest + jnp.log(summed_exp) - jnp.log(jnp.float32(NS))))
    log_coupling = scores + row_potential[:, None] + col_potential[None, :]
    return (log_coupling, row_potential, col_potential)
```

```python
import functools
import math

import jax
import jax.numpy as jnp
from jax import lax
from jax.experimental import pallas as pl
from jax.experimental.pallas import tpu as pltpu
from jax.sharding import PartitionSpec as P

PCS = 50
ITERS = 4
eps_reg = 0.5
marg_power = 1.0 / (1.0 + eps_reg)
tiny_eps = 1e-06
LN2 = math.log(2.0)
LOG2E = 1.0 / LN2

PAD = 64
BLK = 512
HALF = 16
MESH = pl.DeviceIdType.MESH
f32, bf16 = jnp.float32, jnp.bfloat16


def coords():
    s, t = lax.axis_index("src"), lax.axis_index("tgt")
    return t // 8, (s % 2) * 4 + (t // 2) % 4, s // 2, t % 2


def device(x, y, z, c):
    return (z * 2 + y // 4, (x * 4 + y % 4) * 2 + c)


def split3(v):
    hi = v.astype(bf16)
    rest = v - hi.astype(f32)
    mid = rest.astype(bf16)
    lo = (rest - mid.astype(f32)).astype(bf16)
    return jnp.concatenate([hi, mid, lo], axis=0)


def fold3(v):
    n = v.shape[0] // 3
    return (v[:n] + v[n : 2 * n]) + v[2 * n :]


def logsum_pass(table, shift, out):
    chunk = 64

    def step(n, carry):
        tops, sums = carry
        rows = pl.ds(pl.multiple_of(n * chunk, chunk), chunk)
        moved = shift[rows, :].reshape(chunk // 8, 8, 128)
        new_tops, new_sums = [], []
        for j in range(4):
            v = table[rows, j * 128 : (j + 1) * 128].reshape(chunk // 8, 8, 128) + moved
            top = jnp.maximum(tops[j], jnp.max(v, axis=0))
            total = jnp.sum(jnp.exp2(v - top[None]), axis=0)
            new_sums.append(sums[j] * jnp.exp2(tops[j] - top) + total)
            new_tops.append(top)
        return tuple(new_tops), tuple(new_sums)

    start = (
        tuple(jnp.full((8, 128), -1e30, f32) for _ in range(4)),
        tuple(jnp.zeros((8, 128), f32) for _ in range(4)),
    )
    tops, sums = lax.fori_loop(0, table.shape[0] // chunk, step, start, unroll=2)
    for j in range(4):
        top = jnp.max(tops[j], axis=0, keepdims=True)
        total = jnp.sum(sums[j] * jnp.exp2(tops[j] - top), axis=0, keepdims=True)
        out[pl.ds(j, 1), :] = top + jnp.log2(total)


def potentials(slots, halves, log_mass, log_count):
    v = slots.reshape(-1, 2, 4, 128)
    top = jnp.max(v, axis=0)
    total = top + jnp.log2(jnp.sum(jnp.exp2(v - top[None]), axis=0))
    return marg_power * (log_mass - (total - log_count))


def spread(pot, shift):
    flat = jnp.concatenate([pot[0], pot[1]], axis=0)
    turned = jnp.concatenate([flat, jnp.zeros((120, 128), f32)], axis=0).T
    for p in range(8):
        shift[pl.ds(p * 128, 128), :] = jnp.broadcast_to(turned[:, p : p + 1], (128, 128))


def kernel(
    total_rows, total_cols,
    coupling_hbm, src_hbm, tgt_hbm, smass_hbm, tmass_hbm,
    out_ref, row_ref, col_ref,
    coupling, src_in, tgt_in, src_f, tgt_f, smass, tmass,
    src_t, tgt_t, tgt_two, scores, scores_t, shift,
    m0_s, m0_r, m1_s, m1_r, m2_s, m2_r, row_s, row_r, col_s, col_r,
    load_sem, swap_send, swap_recv, m_send, m_recv, row_send, row_recv, col_send, col_recv,
):
    x, y, z, c = coords()
    yh, yl = y // 4, y % 4

    loads = [
        pltpu.make_async_copy(src_hbm, src_in, load_sem.at[0]),
        pltpu.make_async_copy(tgt_hbm, tgt_in, load_sem.at[1]),
        pltpu.make_async_copy(coupling_hbm, coupling, load_sem.at[2]),
        pltpu.make_async_copy(smass_hbm, smass.at[yh], load_sem.at[3]),
        pltpu.make_async_copy(tmass_hbm, tmass.at[c], load_sem.at[4]),
    ]
    for copy in loads:
        copy.start()

    barrier = pltpu.get_barrier_semaphore()
    greeted = 0
    for dx in range(4):
        for dy in (0, 1, 2, 6, 7):
            for core in range(2):
                if (dx, dy) == (0, 0):
                    if core:
                        continue
                    target = device(x, y, z, 1 - c)
                else:
                    target = device((x + dx) % 4, (y + dy) % 8, z, core)
                pl.semaphore_signal(barrier, inc=1, device_id=target, device_id_type=MESH)
                greeted += 1
    for dy in (3, 4, 5):
        pl.semaphore_signal(barrier, inc=1, device_id=device(x, (y + dy) % 8, z, c), device_id_type=MESH)
        greeted += 1
    for dz in range(1, 8):
        for core in range(2):
            pl.semaphore_signal(barrier, inc=1, device_id=device(x, y, (z + dz) % 8, core), device_id_type=MESH)
            greeted += 1

    for ref, own in ((src_f, yh), (tgt_f, c)):
        ref[own, pl.ds(48, 8), :] = jnp.zeros((8, BLK), f32)
        for side in range(2):
            ref[side, pl.ds(56, 8), :] = jnp.zeros((8, BLK), f32)
    for copy in loads[:2]:
        copy.wait()
    src_f[yh, pl.ds(0, PCS), :] = src_in[...].astype(f32)
    tgt_f[c, pl.ds(0, PCS), :] = tgt_in[...].astype(f32)
    tgt_b = tgt_f[c].astype(bf16)
    tgt_two[pl.ds(0, PAD), :] = tgt_b
    tgt_two[pl.ds(PAD, PAD), :] = tgt_b
    shift[...] = jnp.zeros(shift.shape, f32)
    for copy in loads[2:]:
        copy.wait()

    panel = jnp.dot(src_f[yh].astype(bf16), coupling[...], preferred_element_type=f32)
    wide = lax.dot_general(
        split3(panel), tgt_two[...], (((1,), (1,)), ((), ())), preferred_element_type=f32
    )
    wide = fold3(wide)
    left = lax.broadcasted_iota(jnp.int32, (2 * HALF, 128), 1) < PAD
    packed = jnp.where(left, wide[: 2 * HALF], wide[2 * HALF :])
    m0_s[0] = packed[:HALF]
    m0_s[1] = packed[HALF:]
    m0_r[2 * x + c] = jnp.where(c == 0, packed[:HALF], packed[HALF:])

    pl.semaphore_wait(barrier, greeted)

    def send(src, dst, send_sem, recv_sem, target):
        pltpu.make_async_remote_copy(
            src_ref=src, dst_ref=dst, send_sem=send_sem, recv_sem=recv_sem,
            device_id=target, device_id_type=MESH,
        ).start()

    def settle(ref, sem):
        pltpu.make_async_copy(ref, ref, sem).wait()

    for dx in range(4):
        for half in range(2):
            if dx == 0:
                if half:
                    continue
                send(m0_s.at[1 - c], m0_r.at[2 * x + c], m_send.at[0], m_recv.at[0], device(x, y, z, 1 - c))
            else:
                send(m0_s.at[half], m0_r.at[2 * x + c], m_send.at[0], m_recv.at[0], device((x + dx) % 4, y, z, half))

    other = device(x, y, z, 1 - c)
    send(tgt_f.at[c, pl.ds(0, 56)], tgt_f.at[c, pl.ds(0, 56)], swap_send.at[0], swap_recv.at[0], other)
    send(tmass.at[c], tmass.at[c], swap_send.at[1], swap_recv.at[1], other)
    way = jnp.where(yl == 3, 1, 7)

    @pl.when((yl == 0) | (yl == 3))
    def _():
        for far in range(1, 3):
            target = device(x, (y + far * way) % 8, z, c)
            send(src_f.at[yh, pl.ds(0, 56)], src_f.at[yh, pl.ds(0, 56)], swap_send.at[1 + 2 * far - 1], swap_recv.at[2], target)
            send(smass.at[yh], smass.at[yh], swap_send.at[1 + 2 * far], swap_recv.at[3], target)

    settle(m0_r.at[pl.ds(0, 7)], m_recv.at[0])
    part = jnp.sum(m0_r[...], axis=0)
    m1_s[...] = part
    m1_r[y] = part
    for dy in range(1, 8):
        send(m1_s, m1_r.at[y], m_send.at[1], m_recv.at[1], device(x, (y + dy) % 8, z, c))

    settle(tgt_f.at[0, pl.ds(0, 56)], swap_recv.at[0])
    settle(tmass.at[0], swap_recv.at[1])
    zero = jnp.zeros((PAD, BLK), f32)
    for core in range(2):
        rows = tgt_f[core]
        tgt_t[pl.ds(core * BLK, BLK), :] = jnp.concatenate([rows, rows, rows, zero], axis=0).T.astype(bf16)

    settle(m1_r.at[pl.ds(0, 7)], m_recv.at[1])
    part = jnp.sum(m1_r[...], axis=0)
    m2_s[...] = part
    m2_r[2 * z + c] = part
    for dz in range(8):
        for core in range(2):
            if dz == 0:
                if core:
                    continue
                target = other
            else:
                target = device(x, y, (z + dz) % 8, core)
            send(m2_s, m2_r.at[2 * z + c], m_send.at[2], m_recv.at[2], target)

    settle(src_f.at[0, pl.ds(0, 56)], swap_recv.at[2])
    settle(smass.at[0], swap_recv.at[3])
    for side in range(2):
        rows = src_f[side]
        src_t[pl.ds(side * BLK, BLK), :] = jnp.concatenate([rows, rows, rows, zero], axis=0).T.astype(bf16)
    log_src = jnp.log2(smass[...])
    log_tgt = jnp.log2(tmass[...])

    settle(m2_r.at[pl.ds(0, 15)], m_recv.at[2])
    sums = jnp.sum(m2_r[...].reshape(8, 2, HALF, 128), axis=0)
    moment = jnp.concatenate([sums[0], sums[1]], axis=0) * (total_rows * total_cols) ** (-0.5)
    square = jnp.sum(moment * moment, axis=1, keepdims=True)
    square = jnp.sum(square, axis=0, keepdims=True) * (1.0 / (PCS * PCS))
    normed = moment / jnp.sqrt(square + tiny_eps) * (2.0 / (eps_reg * PCS) * LOG2E)

    two = jnp.concatenate([jnp.where(left, normed, 0.0), jnp.where(left, 0.0, normed)], axis=0)
    turned = jnp.concatenate([two, jnp.zeros((PAD, 128), f32)], axis=0).T
    back = turned[:PAD, :PAD] + turned[PAD:, :PAD]
    fill = jnp.zeros((PAD, BLK), bf16)
    weighted = fold3(jnp.dot(split3(two), tgt_two[...], preferred_element_type=f32))
    weighted = jnp.concatenate([split3(weighted), fill], axis=0)
    mine = src_f[c].astype(bf16)
    weighted_t = fold3(jnp.dot(split3(back), mine, preferred_element_type=f32))
    weighted_t = jnp.concatenate([split3(weighted_t), fill], axis=0)
    for n in range(8):
        rows = pl.ds(n * 128, 128)
        scores_t[rows, :] = jnp.dot(tgt_t[rows, :], weighted_t, preferred_element_type=f32)
    for n in range(8):
        rows = pl.ds(n * 128, 128)
        scores[rows, :] = jnp.dot(src_t[rows, :], weighted, preferred_element_type=f32)

    row_slot = 2 * (4 * x + yl) + c
    col_slot = 2 * z + c
    y_two = (y + 2 + 4 * (x % 2)) % 8
    log_rows, log_cols = math.log2(total_rows), math.log2(total_cols)

    def iteration(it, _):
        logsum_pass(scores_t, shift, row_s.at[it])
        row_r[it, row_slot] = row_s[it]
        for dx in range(4):
            for ty in (y, (y + 1) % 8, (y + 7) % 8, y_two):
                for core in range(2):
                    if dx == 0 and ty is y:
                        if core:
                            continue
                        target = other
                    else:
                        target = device((x + dx) % 4, ty, z, core)
                    send(row_s.at[it], row_r.at[it, row_slot], row_send.at[it], row_recv.at[it], target)
        settle(row_r.at[it, pl.ds(0, 31)], row_recv.at[it])
        row_pot = potentials(row_r[it], 16, log_src, log_cols)
        spread(row_pot, shift)
        row_ref[...] = jnp.where(yh == 0, row_pot[0], row_pot[1]) * LN2

        logsum_pass(scores, shift, col_s.at[it])
        col_r[it, col_slot] = col_s[it]
        for dz in range(8):
            for core in range(2):
                if dz == 0:
                    if core:
                        continue
                    target = other
                else:
                    target = device(x, y, (z + dz) % 8, core)
                send(col_s.at[it], col_r.at[it, col_slot], col_send.at[it], col_recv.at[it], target)
        settle(col_r.at[it, pl.ds(0, 15)], col_recv.at[it])
        col_pot = potentials(col_r[it], 8, log_tgt, log_rows)
        col_ref[...] = jnp.where(c == 0, col_pot[0], col_pot[1])

        @pl.when(it == ITERS - 1)
        def _():
            for j in range(4):
                lanes = pl.ds(j * 128, 128)
                add = col_ref[pl.ds(j, 1), :]
                for n in range(8):
                    rows = pl.ds(pl.multiple_of(yh * BLK + n * 64, 64), 64)
                    out_ref[pl.ds(n * 64, 64), lanes] = ((scores[rows, lanes] + shift[rows, :]) + add) * LN2

        spread(col_pot, shift)
        col_ref[...] = col_ref[...] * LN2
        return 0

    lax.fori_loop(0, ITERS, iteration, 0)

    settle(m0_r.at[pl.ds(0, 7)], m_send.at[0])
    settle(m1_r.at[pl.ds(0, 7)], m_send.at[1])
    settle(m2_r.at[pl.ds(0, 15)], m_send.at[2])
    settle(tgt_f.at[0, pl.ds(0, 56)], swap_send.at[0])
    settle(tmass.at[0], swap_send.at[1])

    @pl.when((yl == 0) | (yl == 3))
    def _():
        for far in range(1, 3):
            settle(src_f.at[0, pl.ds(0, 56)], swap_send.at[1 + 2 * far - 1])
            settle(smass.at[0], swap_send.at[1 + 2 * far])

    for it in range(ITERS):
        settle(row_r.at[it, pl.ds(0, 31)], row_send.at[it])
        settle(col_r.at[it, pl.ds(0, 15)], col_send.at[it])


def shards(coupling, src_pcs, tgt_pcs, src_mass, tgt_mass):
    total_rows = coupling.shape[0] * lax.axis_size("src")
    total_cols = coupling.shape[1] * lax.axis_size("tgt")
    dma = pltpu.SemaphoreType.DMA
    vec = lambda *lead: pltpu.VMEM((*lead, 4, 128), f32)
    out, row, col = pl.pallas_call(
        functools.partial(kernel, total_rows, total_cols),
        out_shape=(
            jax.ShapeDtypeStruct((BLK, BLK), f32),
            jax.ShapeDtypeStruct((4, 128), f32),
            jax.ShapeDtypeStruct((4, 128), f32),
        ),
        in_specs=[pl.BlockSpec(memory_space=pl.ANY)] * 5,
        out_specs=[pl.BlockSpec(memory_space=pltpu.VMEM)] * 3,
        scratch_shapes=[
            pltpu.VMEM((BLK, BLK), bf16),
            pltpu.VMEM((PCS, BLK), bf16),
            pltpu.VMEM((PCS, BLK), bf16),
            pltpu.VMEM((2, PAD, BLK), f32),
            pltpu.VMEM((2, PAD, BLK), f32),
            vec(2),
            vec(2),
            pltpu.VMEM((2 * BLK, 4 * PAD), bf16),
            pltpu.VMEM((2 * BLK, 4 * PAD), bf16),
            pltpu.VMEM((2 * PAD, BLK), bf16),
            pltpu.VMEM((2 * BLK, BLK), f32),
            pltpu.VMEM((2 * BLK, BLK), f32),
            pltpu.VMEM((2 * BLK, 128), f32),
            pltpu.VMEM((2, HALF, 128), f32),
            pltpu.VMEM((8, HALF, 128), f32),
            pltpu.VMEM((HALF, 128), f32),
            pltpu.VMEM((8, HALF, 128), f32),
            pltpu.VMEM((HALF, 128), f32),
            pltpu.VMEM((16, HALF, 128), f32),
            vec(ITERS),
            vec(ITERS, 32),
            vec(ITERS),
            vec(ITERS, 16),
            dma((5,)),
            dma((6,)),
            dma((4,)),
            dma((3,)),
            dma((3,)),
            dma((ITERS,)),
            dma((ITERS,)),
            dma((ITERS,)),
            dma((ITERS,)),
        ],
        compiler_params=pltpu.CompilerParams(collective_id=0, has_side_effects=True),
        name="coupling_step",
    )(coupling, src_pcs, tgt_pcs, src_mass.reshape(4, 128), tgt_mass.reshape(4, 128))
    return out, row.reshape(-1), col.reshape(-1)


def solution(mesh):
    in_specs = (P("src", "tgt"), P(None, "src"), P(None, "tgt"), P("src"), P("tgt"))
    out_specs = (P("src", "tgt"), P("src"), P("tgt"))
    return jax.shard_map(shards, mesh=mesh, in_specs=in_specs, out_specs=out_specs, check_vma=False)
```

```python
import functools
import math

import jax
import jax.numpy as jnp
from jax import lax
from jax.experimental import pallas as pl
from jax.experimental.pallas import tpu as pltpu
from jax.sharding import PartitionSpec as P

PCS = 50
ITERS = 4
eps_reg = 0.5
marg_power = 1.0 / (1.0 + eps_reg)
tiny_eps = 1e-06
LN2 = math.log(2.0)
LOG2E = 1.0 / LN2

PAD = 64
SENT = 56
BLK = 512
TWO = 2 * BLK
MESH = pl.DeviceIdType.MESH
f32, bf16 = jnp.float32, jnp.bfloat16
FAR_X, FAR_8 = (2, 1, 3), (4, 3, 5, 2, 6, 1, 7)


def coords():
    s, t = lax.axis_index("src"), lax.axis_index("tgt")
    return t // 8, (s % 2) * 4 + (t // 2) % 4, s // 2, t % 2


def device(x, y, z, c):
    return (z * 2 + y // 4, (x * 4 + y % 4) * 2 + c)


def split3(v):
    hi = v.astype(bf16)
    rest = v - hi.astype(f32)
    mid = rest.astype(bf16)
    lo = (rest - mid.astype(f32)).astype(bf16)
    return jnp.concatenate([hi, mid, lo], axis=0)


def fold3(v):
    n = v.shape[0] // 3
    return (v[:n] + v[n : 2 * n]) + v[2 * n :]


def thrice(v):
    return jnp.concatenate([v, v, v, jnp.zeros_like(v)], axis=0).T.astype(bf16)


def stack4(v):
    terms = split3(v)
    return jnp.concatenate([terms, jnp.zeros((PAD, v.shape[1]), bf16)], axis=0)


def turn(pot):
    return jnp.concatenate([pot, jnp.zeros((120, 128), f32)], axis=0).T


def logsum_pass(table, pot, shift, out):
    turned = turn(pot)
    for pair in range(4):
        tops = [jnp.full((8, 128), -1e30, f32)] * 2
        sums = [jnp.zeros((8, 128), f32)] * 2
        for p in range(8):
            rows = pl.ds(p * 128, 128)
            if pair == 0:
                moved = jnp.broadcast_to(turned[:, p : p + 1], (128, 128))
                shift[rows, :] = moved
            else:
                moved = shift[rows, :]
            moved = moved.reshape(16, 8, 128)
            for k in range(2):
                j = 2 * pair + k
                v = table[rows, j * 128 : (j + 1) * 128].reshape(16, 8, 128) + moved
                top = jnp.maximum(tops[k], jnp.max(v, axis=0))
                total = jnp.sum(jnp.exp2(v - top[None]), axis=0)
                sums[k] = sums[k] * jnp.exp2(tops[k] - top) + total
                tops[k] = top
        for k in range(2):
            top = jnp.max(tops[k], axis=0, keepdims=True)
            total = jnp.sum(sums[k] * jnp.exp2(tops[k] - top), axis=0, keepdims=True)
            out[pl.ds(2 * pair + k, 1), :] = top + jnp.log2(total)


def potentials(v, log_mass, log_count):
    top = jnp.max(v, axis=0)
    total = top + jnp.log2(jnp.sum(jnp.exp2(v - top[None]), axis=0))
    return marg_power * (log_mass - (total - log_count))


def send(src, dst, send_sem, recv_sem, target):
    pltpu.make_async_remote_copy(
        src_ref=src, dst_ref=dst, send_sem=send_sem, recv_sem=recv_sem,
        device_id=target, device_id_type=MESH,
    ).start()


def settle(ref, sem):
    pltpu.make_async_copy(ref, ref, sem).wait()


def greet(targets):
    barrier = pltpu.get_barrier_semaphore()
    for target in targets:
        pl.semaphore_signal(barrier, inc=1, device_id=target, device_id_type=MESH)


def kernel(
    total_rows, total_cols,
    coupling_hbm, src_hbm, tgt_hbm, smass_hbm, tmass_hbm,
    sum_ref, row_ref, col_ref,
    coupling, src_in, tgt_in, src_b, tgt_two, src_f, tgt_f, smass, tmass,
    src_t, tgt_t, src_all, tgt_all, scores, scores_t, shift, pot,
    m0_s, m0_r, m1_s, m1_r, m2_s, m2_r, nrm, row_s, row_r, col_s, col_r, fin_s,
    load_sem, swap_send, swap_recv, m_send, m_recv, row_send, row_recv, col_send, col_recv, fin_send, fin_recv,
):
    x, y, z, c = coords()
    yh, yl = y // 4, y % 4
    on_one, on_zero = c == 1, c == 0

    loads = [
        pltpu.make_async_copy(src_hbm, src_in, load_sem.at[0]),
        pltpu.make_async_copy(tgt_hbm, tgt_in, load_sem.at[1]),
        pltpu.make_async_copy(coupling_hbm, coupling, load_sem.at[2]),
        pltpu.make_async_copy(smass_hbm, smass.at[yh], load_sem.at[3]),
        pltpu.make_async_copy(tmass_hbm, tmass.at[c], load_sem.at[4]),
    ]
    for copy in loads:
        copy.start()

    row_peers = [(dx, dy) for dx in (2, 1, 3, 0) for dy in (2, 6, 1, 7)]
    ones = [device((x + dx) % 4, (y + dy) % 8, z, 1) for dx, dy in row_peers]
    ones += [device((x + dx) % 4, y, z, 1) for dx in FAR_X]
    ones += [device(x, (y + dy) % 8, z, 1) for dy in (4, 3, 5)]
    ones += [device(x, y, (z + dz) % 8, 1) for dz in FAR_8]
    near = [device((x + dx) % 4, y, z, 0) for dx in (2, 1, 3, 0)]

    @pl.when(on_one)
    def _():
        greet(ones + near)

    @pl.when(on_zero)
    def _():
        greet([device(x, y, (z + dz) % 8, 1) for dz in FAR_8])
        greet([device((x + dx) % 4, y, z, 1) for dx in (2, 1, 3, 0)])

    src_b[pl.ds(48, 16), :] = jnp.zeros((16, BLK), bf16)
    tgt_two[pl.ds(48, 16), :] = jnp.zeros((16, BLK), bf16)
    tgt_two[pl.ds(112, 16), :] = jnp.zeros((16, BLK), bf16)
    for copy in loads[:2]:
        copy.wait()
    src_b[pl.ds(0, PCS), :] = src_in[...]
    tgt_two[pl.ds(0, PCS), :] = tgt_in[...]
    tgt_two[pl.ds(PAD, PCS), :] = tgt_in[...]
    loads[2].wait()

    panel = jnp.dot(src_b[...], coupling[...], preferred_element_type=f32)
    wide = fold3(
        lax.dot_general(
            split3(panel), tgt_two[...], (((1,), (1,)), ((), ())), preferred_element_type=f32
        )
    )
    left = lax.broadcasted_iota(jnp.int32, (32, 128), 1) < PAD
    packed = jnp.where(left, wide[:32], wide[32:])
    m0_s[...] = packed

    barrier = pltpu.get_barrier_semaphore()
    own0 = 2 * x + c

    @pl.when(on_one)
    def _():
        pl.semaphore_wait(barrier, len(ones) + 7 + 4)
        m0_r[own0] = packed
        for dx in FAR_X:
            send(m0_s, m0_r.at[own0], m_send.at[0], m_recv.at[0], device((x + dx) % 4, y, z, 1))

    @pl.when(on_zero)
    def _():
        pl.semaphore_wait(barrier, 4)
        for dx in (2, 1, 3, 0):
            send(m0_s, m0_r.at[own0], m_send.at[0], m_recv.at[0], device((x + dx) % 4, y, z, 1))

    for ref, own, block in ((src_f, yh, src_b), (tgt_f, c, tgt_two)):
        for side in range(2):
            ref[side, pl.ds(SENT, 8), :] = jnp.zeros((8, BLK), f32)
        ref[own, pl.ds(0, SENT), :] = block[pl.ds(0, PAD), :].astype(f32)[:SENT]
    for copy in loads[3:]:
        copy.wait()

    rows56 = pl.ds(0, SENT)

    def normed_of(packed_sum):
        moment = packed_sum * (total_rows * total_cols) ** (-0.5)
        square = jnp.sum(moment * moment, axis=1, keepdims=True)
        square = jnp.sum(square, axis=0, keepdims=True) * (1.0 / (PCS * PCS))
        scaled = moment / jnp.sqrt(square + tiny_eps) * (2.0 / (eps_reg * PCS) * LOG2E)
        return jnp.concatenate([jnp.where(left, scaled, 0.0), jnp.where(left, 0.0, scaled)], axis=0)

    log_rows, log_cols = math.log2(total_rows), math.log2(total_cols)
    partner = device(x, y, z, 1 - c)
    last = ITERS - 1

    @pl.when(on_zero)
    def _():
        send(tgt_f.at[0, rows56], tgt_f.at[0, rows56], swap_send.at[0], swap_recv.at[0], partner)
        send(tmass.at[0], tmass.at[0], swap_send.at[1], swap_recv.at[1], partner)
        src_t[pl.ds(0, BLK), :] = thrice(src_f[yh])
        log_tgt = jnp.log2(tmass[0])

        settle(nrm, fin_recv.at[0])
        weighted = fold3(jnp.dot(split3(normed_of(nrm[...])), tgt_two[...], preferred_element_type=f32))
        sum_ref[...] = jnp.dot(src_t[pl.ds(0, BLK), :], stack4(weighted), preferred_element_type=f32)

        settle(pot, fin_recv.at[1])
        half = jnp.where(yh == 0, pot[pl.ds(0, 4), :], pot[pl.ds(4, 4), :])
        row_ref[...] = half * LN2
        turned = turn(jnp.concatenate([half, jnp.zeros((4, 128), f32)], axis=0))
        for p in range(4):
            rows = pl.ds(p * 128, 128)
            moved = jnp.broadcast_to(turned[:, p : p + 1], (128, 128))
            for j in range(4):
                lanes = pl.ds(j * 128, 128)
                sum_ref[rows, lanes] = sum_ref[rows, lanes] + moved

        settle(col_r.at[last], col_recv.at[last])
        col_ref[...] = potentials(col_r[last][:, :4, :], log_tgt, log_rows)

        settle(m0_r.at[pl.ds(0, 4)], m_send.at[0])
        settle(tgt_f.at[0, rows56], swap_send.at[0])
        settle(tmass.at[0], swap_send.at[1])

    edge = (yl == 0) | (yl == 3)

    @pl.when(on_one & edge)
    def _():
        way = jnp.where(yl == 3, 1, 7)
        for far in range(1, 3):
            target = device(x, (y + far * way) % 8, z, 1)
            send(src_f.at[yh, rows56], src_f.at[yh, rows56], swap_send.at[2 * far - 2], swap_recv.at[2], target)
            send(smass.at[yh], smass.at[yh], swap_send.at[2 * far - 1], swap_recv.at[3], target)

    @pl.when(on_one)
    def _():
        tgt_t[pl.ds(BLK, BLK), :] = thrice(tgt_f[1])

        settle(m0_r.at[pl.ds(0, 7)], m_recv.at[0])
        part = jnp.sum(m0_r[...], axis=0)
        m1_s[...] = part
        for dy in FAR_8:
            send(m1_s, m1_r.at[y], m_send.at[1], m_recv.at[1], device(x, (y + dy) % 8, z, 1))
        m1_r[y] = part

        settle(tgt_f.at[0, rows56], swap_recv.at[0])
        settle(tmass.at[0], swap_recv.at[1])
        tgt_t[pl.ds(0, BLK), :] = thrice(tgt_f[0])
        near_b = tgt_f[0].astype(bf16)
        tgt_all[pl.ds(0, PAD), pl.ds(0, BLK)] = near_b
        tgt_all[pl.ds(PAD, PAD), pl.ds(0, BLK)] = near_b
        tgt_all[:, pl.ds(BLK, BLK)] = tgt_two[...]

        settle(m1_r.at[pl.ds(0, 7)], m_recv.at[1])
        part = jnp.sum(m1_r[...], axis=0)
        m2_s[...] = part
        for dz in FAR_8:
            send(m2_s, m2_r.at[z], m_send.at[2], m_recv.at[2], device(x, y, (z + dz) % 8, 1))
        m2_r[z] = part

        settle(src_f.at[0, rows56], swap_recv.at[2])
        settle(smass.at[0], swap_recv.at[3])
        for side in range(2):
            src_t[pl.ds(side * BLK, BLK), :] = thrice(src_f[side])
            src_all[:, pl.ds(side * BLK, BLK)] = src_f[side].astype(bf16)
        log_src = jnp.log2(jnp.concatenate([smass[0], smass[1]], axis=0))
        log_tgt = jnp.log2(jnp.concatenate([tmass[0], tmass[1]], axis=0))
        pot[...] = jnp.zeros((8, 128), f32)

        settle(m2_r.at[pl.ds(0, 7)], m_recv.at[2])
        total = jnp.sum(m2_r[...], axis=0)
        nrm[...] = total
        send(nrm, nrm, fin_send.at[0], fin_recv.at[0], partner)

        two = normed_of(total)
        turned = jnp.concatenate([two, jnp.zeros((PAD, 128), f32)], axis=0).T
        back = turned[:PAD, :PAD] + turned[PAD:, :PAD]
        weighted_t = stack4(fold3(jnp.dot(split3(back), src_all[...], preferred_element_type=f32)))
        for n in range(8):
            rows = pl.ds(n * 128, 128)
            scores_t[rows, :] = jnp.dot(tgt_t[rows, :], weighted_t, preferred_element_type=f32)

        row_slot = 4 * x + yl
        y_two = (y + 2 + 4 * (x % 2)) % 8

        def iteration(it, _):
            logsum_pass(scores_t, pot[...], shift, row_s.at[it])
            for dx in (2, 1, 3, 0):
                for ty in (y_two, (y + 1) % 8, (y + 7) % 8, y):
                    if dx or ty is not y:
                        target = device((x + dx) % 4, ty, z, 1)
                        send(row_s.at[it], row_r.at[it, row_slot], row_send.at[it], row_recv.at[it], target)
            row_r[it, row_slot] = row_s[it]

            @pl.when(it == 0)
            def _():
                weighted = stack4(fold3(jnp.dot(split3(two), tgt_all[...], preferred_element_type=f32)))
                for n in range(8):
                    rows = pl.ds(n * 128, 128)
                    scores[rows, :] = jnp.dot(src_t[rows, :], weighted, preferred_element_type=f32)

            settle(row_r.at[it, pl.ds(0, 15)], row_recv.at[it])
            row_pot = potentials(row_r[it], log_src, log_cols)
            pot[...] = row_pot

            @pl.when(it == last)
            def _():
                fin_s[...] = row_pot
                send(fin_s, pot, fin_send.at[1], fin_recv.at[1], partner)

            logsum_pass(scores, row_pot, shift, col_s.at[it])
            for dz in FAR_8:
                send(col_s.at[it], col_r.at[it, z], col_send.at[it], col_recv.at[it], device(x, y, (z + dz) % 8, 1))
            col_r[it, z] = col_s[it]

            @pl.when(it == last)
            def _():
                for dz in (*FAR_8, 0):
                    target = device(x, y, (z + dz) % 8, 0)
                    send(col_s.at[it], col_r.at[it, z], fin_send.at[2], col_recv.at[it], target)
                row_ref[...] = jnp.where(yh == 0, row_pot[:4], row_pot[4:]) * LN2
                for n in range(4):
                    to = pl.ds(n * 128, 128)
                    rows = pl.ds(pl.multiple_of(yh * BLK + n * 128, 128), 128)
                    moved = shift[rows, :]
                    for j in range(4):
                        sum_ref[to, pl.ds(j * 128, 128)] = scores[rows, pl.ds(BLK + j * 128, 128)] + moved

            settle(col_r.at[it, pl.ds(0, 7)], col_recv.at[it])
            pot[...] = potentials(col_r[it], log_tgt, log_rows)
            return 0

        lax.fori_loop(0, ITERS, iteration, 0)
        col_ref[...] = pot[pl.ds(4, 4), :]

        settle(m0_r.at[pl.ds(0, 3)], m_send.at[0])
        settle(m1_r.at[pl.ds(0, 7)], m_send.at[1])
        settle(m2_r.at[pl.ds(0, 7)], m_send.at[2])
        settle(nrm, fin_send.at[0])
        settle(fin_s, fin_send.at[1])
        settle(col_r.at[last], fin_send.at[2])
        for it in range(ITERS):
            settle(row_r.at[it, pl.ds(0, 15)], row_send.at[it])
            settle(col_r.at[it, pl.ds(0, 7)], col_send.at[it])

    @pl.when(on_one & edge)
    def _():
        for far in range(1, 3):
            settle(src_f.at[0, rows56], swap_send.at[2 * far - 2])
            settle(smass.at[0], swap_send.at[2 * far - 1])


def finish(sum_ref, row_in, col_in, out_hbm, row_ref, col_ref, tile, sem):
    copies = []
    for n in range(8):
        rows = pl.ds(n * 64, 64)
        for j in range(4):
            lanes = pl.ds(j * 128, 128)
            tile[rows, lanes] = (sum_ref[rows, lanes] + col_in[pl.ds(j, 1), :]) * LN2
        copies.append(pltpu.make_async_copy(tile.at[rows], out_hbm.at[rows], sem.at[n]))
        copies[-1].start()
    row_ref[...] = row_in[...]
    col_ref[...] = col_in[...] * LN2
    for copy in copies:
        copy.wait()


def shards(coupling, src_pcs, tgt_pcs, src_mass, tgt_mass):
    total_rows = coupling.shape[0] * lax.axis_size("src")
    total_cols = coupling.shape[1] * lax.axis_size("tgt")
    dma = pltpu.SemaphoreType.DMA
    full, vec = jax.ShapeDtypeStruct((BLK, BLK), f32), jax.ShapeDtypeStruct((4, 128), f32)
    in_vmem, anywhere = pl.BlockSpec(memory_space=pltpu.VMEM), pl.BlockSpec(memory_space=pl.ANY)
    tile = lambda *lead: pltpu.VMEM((*lead, 8, 128), f32)
    gram = lambda *lead: pltpu.VMEM((*lead, 32, 128), f32)
    sums, row, col = pl.pallas_call(
        functools.partial(kernel, total_rows, total_cols),
        out_shape=(full, vec, vec),
        in_specs=[anywhere] * 5,
        out_specs=[in_vmem] * 3,
        scratch_shapes=[
            pltpu.VMEM((BLK, BLK), bf16),
            pltpu.VMEM((PCS, BLK), bf16),
            pltpu.VMEM((PCS, BLK), bf16),
            pltpu.VMEM((PAD, BLK), bf16),
            pltpu.VMEM((2 * PAD, BLK), bf16),
            pltpu.VMEM((2, PAD, BLK), f32),
            pltpu.VMEM((2, PAD, BLK), f32),
            pltpu.VMEM((2, 4, 128), f32),
            pltpu.VMEM((2, 4, 128), f32),
            pltpu.VMEM((TWO, 4 * PAD), bf16),
            pltpu.VMEM((TWO, 4 * PAD), bf16),
            pltpu.VMEM((PAD, TWO), bf16),
            pltpu.VMEM((2 * PAD, TWO), bf16),
            pltpu.VMEM((TWO, TWO), f32),
            pltpu.VMEM((TWO, TWO), f32),
            pltpu.VMEM((TWO, 128), f32),
            tile(),
            gram(),
            gram(8),
            gram(),
            gram(8),
            gram(),
            gram(8),
            gram(),
            tile(ITERS),
            tile(ITERS, 16),
            tile(ITERS),
            tile(ITERS, 8),
            tile(),
            dma((5,)),
            dma((4,)),
            dma((4,)),
            dma((3,)),
            dma((3,)),
            dma((ITERS,)),
            dma((ITERS,)),
            dma((ITERS,)),
            dma((ITERS,)),
            dma((3,)),
            dma((3,)),
        ],
        compiler_params=pltpu.CompilerParams(collective_id=0, has_side_effects=True),
        name="coupling_step",
    )(coupling, src_pcs, tgt_pcs, src_mass.reshape(4, 128), tgt_mass.reshape(4, 128))
    out, row, col = pl.pallas_call(
        finish,
        out_shape=(full, vec, vec),
        in_specs=[in_vmem] * 3,
        out_specs=[anywhere, in_vmem, in_vmem],
        scratch_shapes=[pltpu.VMEM((BLK, BLK), f32), dma((8,))],
        name="finish",
    )(sums, row, col)
    return out, row.reshape(-1), col.reshape(-1)


def solution(mesh):
    in_specs = (P("src", "tgt"), P(None, "src"), P(None, "tgt"), P("src"), P("tgt"))
    out_specs = (P("src", "tgt"), P("src"), P("tgt"))
    return jax.shard_map(shards, mesh=mesh, in_specs=in_specs, out_specs=out_specs, check_vma=False)
```

```python
import functools
import math

import jax
import jax.numpy as jnp
from jax import lax
from jax.experimental import pallas as pl
from jax.experimental.pallas import tpu as pltpu
from jax.sharding import PartitionSpec as P

PCS = 50
ITERS = 4
eps_reg = 0.5
marg_power = 1.0 / (1.0 + eps_reg)
tiny_eps = 1e-06
LN2 = math.log(2.0)
LOG2E = 1.0 / LN2

PAD = 64
SENT = 56
BLK = 512
TWO = 2 * BLK
MESH = pl.DeviceIdType.MESH
f32, bf16 = jnp.float32, jnp.bfloat16
FAR_X, FAR_8 = (2, 1, 3), (4, 3, 5, 2, 6, 1, 7)


def coords():
    s, t = lax.axis_index("src"), lax.axis_index("tgt")
    return t // 8, (s % 2) * 4 + (t // 2) % 4, s // 2, t % 2


def device(x, y, z, c):
    return (z * 2 + y // 4, (x * 4 + y % 4) * 2 + c)


def split3(v):
    hi = v.astype(bf16)
    rest = v - hi.astype(f32)
    mid = rest.astype(bf16)
    lo = (rest - mid.astype(f32)).astype(bf16)
    return jnp.concatenate([hi, mid, lo], axis=0)


def fold3(v):
    n = v.shape[0] // 3
    return (v[:n] + v[n : 2 * n]) + v[2 * n :]


def thrice(v):
    return jnp.concatenate([v, v, v, jnp.zeros_like(v)], axis=0).T.astype(bf16)


def stack4(v):
    terms = split3(v)
    return jnp.concatenate([terms, jnp.zeros((PAD, v.shape[1]), bf16)], axis=0)


def turn(pot):
    return jnp.concatenate([pot, jnp.zeros((120, 128), f32)], axis=0).T


def logsum_pass(table, pot, shift, out):
    turned = turn(pot)
    for pair in range(4):
        tops = [jnp.full((8, 128), -1e30, f32)] * 2
        sums = [jnp.zeros((8, 128), f32)] * 2
        for p in range(8):
            rows = pl.ds(p * 128, 128)
            if pair == 0:
                moved = jnp.broadcast_to(turned[:, p : p + 1], (128, 128))
                shift[rows, :] = moved
            else:
                moved = shift[rows, :]
            moved = moved.reshape(16, 8, 128)
            for k in range(2):
                j = 2 * pair + k
                v = table[rows, j * 128 : (j + 1) * 128].reshape(16, 8, 128) + moved
                top = jnp.maximum(tops[k], jnp.max(v, axis=0))
                total = jnp.sum(jnp.exp2(v - top[None]), axis=0)
                sums[k] = sums[k] * jnp.exp2(tops[k] - top) + total
                tops[k] = top
        for k in range(2):
            top = jnp.max(tops[k], axis=0, keepdims=True)
            total = jnp.sum(sums[k] * jnp.exp2(tops[k] - top), axis=0, keepdims=True)
            out[pl.ds(2 * pair + k, 1), :] = top + jnp.log2(total)


def potentials(v, log_mass, log_count):
    top = jnp.max(v, axis=0)
    total = top + jnp.log2(jnp.sum(jnp.exp2(v - top[None]), axis=0))
    return marg_power * (log_mass - (total - log_count))


def send(src, dst, send_sem, recv_sem, target):
    pltpu.make_async_remote_copy(
        src_ref=src, dst_ref=dst, send_sem=send_sem, recv_sem=recv_sem,
        device_id=target, device_id_type=MESH,
    ).start()


def settle(ref, sem):
    pltpu.make_async_copy(ref, ref, sem).wait()


def greet(targets):
    barrier = pltpu.get_barrier_semaphore()
    for target in targets:
        pl.semaphore_signal(barrier, inc=1, device_id=target, device_id_type=MESH)


def kernel(
    total_rows, total_cols,
    coupling_hbm, src_hbm, tgt_hbm, smass_hbm, tmass_hbm,
    sum_ref, row_ref, col_ref,
    coupling, src_in, tgt_in, src_b, tgt_two, src_f, tgt_f, smass, tmass,
    src_t, tgt_t, src_all, tgt_all, scores, scores_t, shift, pot,
    m0_s, m0_r, m1_s, m1_r, m2_s, m2_r, nrm, row_s, row_r, col_s, col_r, fin_s,
    load_sem, swap_send, swap_recv, m_send, m_recv, row_send, row_recv, col_send, col_recv, fin_send, fin_recv,
):
    x, y, z, c = coords()
    yh, yl = y // 4, y % 4
    on_one, on_zero = c == 1, c == 0

    loads = [
        pltpu.make_async_copy(src_hbm, src_in, load_sem.at[0]),
        pltpu.make_async_copy(tgt_hbm, tgt_in, load_sem.at[1]),
        pltpu.make_async_copy(coupling_hbm, coupling, load_sem.at[2]),
        pltpu.make_async_copy(smass_hbm, smass.at[yh], load_sem.at[3]),
        pltpu.make_async_copy(tmass_hbm, tmass.at[c], load_sem.at[4]),
    ]
    for copy in loads:
        copy.start()

    row_peers = [(dx, dy) for dx in (2, 1, 3, 0) for dy in (2, 6, 1, 7)]
    ones = [device((x + dx) % 4, (y + dy) % 8, z, 1) for dx, dy in row_peers]
    ones += [device((x + dx) % 4, y, z, 1) for dx in FAR_X]
    ones += [device(x, (y + dy) % 8, z, 1) for dy in (4, 3, 5)]
    ones += [device(x, y, (z + dz) % 8, 1) for dz in FAR_8]
    near = [device((x + dx) % 4, y, z, 0) for dx in (2, 1, 3, 0)]

    @pl.when(on_one)
    def _():
        greet(ones + near)

    @pl.when(on_zero)
    def _():
        greet([device(x, y, (z + dz) % 8, 1) for dz in FAR_8])
        greet([device((x + dx) % 4, y, z, 1) for dx in (2, 1, 3, 0)])

    src_b[pl.ds(48, 16), :] = jnp.zeros((16, BLK), bf16)
    tgt_two[pl.ds(48, 16), :] = jnp.zeros((16, BLK), bf16)
    tgt_two[pl.ds(112, 16), :] = jnp.zeros((16, BLK), bf16)
    for copy in loads[:2]:
        copy.wait()
    src_b[pl.ds(0, PCS), :] = src_in[...]
    tgt_two[pl.ds(0, PCS), :] = tgt_in[...]
    tgt_two[pl.ds(PAD, PCS), :] = tgt_in[...]
    loads[2].wait()

    panel = jnp.dot(src_b[...], coupling[...], preferred_element_type=f32)
    wide = fold3(
        lax.dot_general(
            split3(panel), tgt_two[...], (((1,), (1,)), ((), ())), preferred_element_type=f32
        )
    )
    left = lax.broadcasted_iota(jnp.int32, (32, 128), 1) < PAD
    packed = jnp.where(left, wide[:32], wide[32:])
    m0_s[...] = packed

    barrier = pltpu.get_barrier_semaphore()
    own0 = 2 * x + c

    @pl.when(on_one)
    def _():
        pl.semaphore_wait(barrier, len(ones) + 7 + 4)
        m0_r[own0] = packed
        for dx in FAR_X:
            send(m0_s, m0_r.at[own0], m_send.at[0], m_recv.at[0], device((x + dx) % 4, y, z, 1))

    @pl.when(on_zero)
    def _():
        pl.semaphore_wait(barrier, 4)
        for dx in (2, 1, 3, 0):
            send(m0_s, m0_r.at[own0], m_send.at[0], m_recv.at[0], device((x + dx) % 4, y, z, 1))

    for ref, own, block in ((src_f, yh, src_b), (tgt_f, c, tgt_two)):
        for side in range(2):
            ref[side, pl.ds(SENT, 8), :] = jnp.zeros((8, BLK), f32)
        ref[own, pl.ds(0, SENT), :] = block[pl.ds(0, PAD), :].astype(f32)[:SENT]
    for copy in loads[3:]:
        copy.wait()

    rows56 = pl.ds(0, SENT)

    def normed_of(packed_sum):
        moment = packed_sum * (total_rows * total_cols) ** (-0.5)
        square = jnp.sum(moment * moment, axis=1, keepdims=True)
        square = jnp.sum(square, axis=0, keepdims=True) * (1.0 / (PCS * PCS))
        scaled = moment / jnp.sqrt(square + tiny_eps) * (2.0 / (eps_reg * PCS) * LOG2E)
        return jnp.concatenate([jnp.where(left, scaled, 0.0), jnp.where(left, 0.0, scaled)], axis=0)

    log_rows, log_cols = math.log2(total_rows), math.log2(total_cols)
    partner = device(x, y, z, 1 - c)
    last = ITERS - 1

    @pl.when(on_zero)
    def _():
        send(tgt_f.at[0, rows56], tgt_f.at[0, rows56], swap_send.at[0], swap_recv.at[0], partner)
        send(tmass.at[0], tmass.at[0], swap_send.at[1], swap_recv.at[1], partner)
        src_t[pl.ds(0, BLK), :] = thrice(src_f[yh])
        log_tgt = jnp.log2(tmass[0])

        settle(nrm, fin_recv.at[0])
        weighted = fold3(jnp.dot(split3(normed_of(nrm[...])), tgt_two[...], preferred_element_type=f32))
        sum_ref[...] = jnp.dot(src_t[pl.ds(0, BLK), :], stack4(weighted), preferred_element_type=f32)

        settle(pot, fin_recv.at[1])
        half = jnp.where(yh == 0, pot[pl.ds(0, 4), :], pot[pl.ds(4, 4), :])
        row_ref[...] = half * LN2
        turned = turn(jnp.concatenate([half, jnp.zeros((4, 128), f32)], axis=0))
        for p in range(4):
            rows = pl.ds(p * 128, 128)
            moved = jnp.broadcast_to(turned[:, p : p + 1], (128, 128))
            for j in range(4):
                lanes = pl.ds(j * 128, 128)
                sum_ref[rows, lanes] = sum_ref[rows, lanes] + moved

        settle(col_r.at[last], col_recv.at[last])
        col_ref[...] = potentials(col_r[last][:, :4, :], log_tgt, log_rows)

        settle(m0_r.at[pl.ds(0, 4)], m_send.at[0])
        settle(tgt_f.at[0, rows56], swap_send.at[0])
        settle(tmass.at[0], swap_send.at[1])

    edge = (yl == 0) | (yl == 3)

    @pl.when(on_one & edge)
    def _():
        way = jnp.where(yl == 3, 1, 7)
        for far in range(1, 3):
            target = device(x, (y + far * way) % 8, z, 1)
            send(src_f.at[yh, rows56], src_f.at[yh, rows56], swap_send.at[2 * far - 2], swap_recv.at[2], target)
            send(smass.at[yh], smass.at[yh], swap_send.at[2 * far - 1], swap_recv.at[3], target)

    @pl.when(on_one)
    def _():
        tgt_t[pl.ds(BLK, BLK), :] = thrice(tgt_f[1])

        settle(m0_r.at[pl.ds(0, 7)], m_recv.at[0])
        part = jnp.sum(m0_r[...], axis=0)
        m1_s[...] = part
        for dy in FAR_8:
            send(m1_s, m1_r.at[y], m_send.at[1], m_recv.at[1], device(x, (y + dy) % 8, z, 1))
        m1_r[y] = part

        settle(tgt_f.at[0, rows56], swap_recv.at[0])
        settle(tmass.at[0], swap_recv.at[1])
        tgt_t[pl.ds(0, BLK), :] = thrice(tgt_f[0])
        near_b = tgt_f[0].astype(bf16)
        tgt_all[pl.ds(0, PAD), pl.ds(0, BLK)] = near_b
        tgt_all[pl.ds(PAD, PAD), pl.ds(0, BLK)] = near_b
        tgt_all[:, pl.ds(BLK, BLK)] = tgt_two[...]

        settle(m1_r.at[pl.ds(0, 7)], m_recv.at[1])
        part = jnp.sum(m1_r[...], axis=0)
        m2_s[...] = part
        for dz in FAR_8:
            send(m2_s, m2_r.at[z], m_send.at[2], m_recv.at[2], device(x, y, (z + dz) % 8, 1))
        m2_r[z] = part

        settle(src_f.at[0, rows56], swap_recv.at[2])
        settle(smass.at[0], swap_recv.at[3])
        for side in range(2):
            src_t[pl.ds(side * BLK, BLK), :] = thrice(src_f[side])
            src_all[:, pl.ds(side * BLK, BLK)] = src_f[side].astype(bf16)
        log_src = jnp.log2(jnp.concatenate([smass[0], smass[1]], axis=0))
        log_tgt = jnp.log2(jnp.concatenate([tmass[0], tmass[1]], axis=0))
        pot[...] = jnp.zeros((8, 128), f32)

        settle(m2_r.at[pl.ds(0, 7)], m_recv.at[2])
        total = jnp.sum(m2_r[...], axis=0)
        nrm[...] = total
        send(nrm, nrm, fin_send.at[0], fin_recv.at[0], partner)

        two = normed_of(total)
        turned = jnp.concatenate([two, jnp.zeros((PAD, 128), f32)], axis=0).T
        back = turned[:PAD, :PAD] + turned[PAD:, :PAD]
        weighted_t = stack4(fold3(jnp.dot(split3(back), src_all[...], preferred_element_type=f32)))
        for n in range(8):
            rows = pl.ds(n * 128, 128)
            scores_t[rows, :] = jnp.dot(tgt_t[rows, :], weighted_t, preferred_element_type=f32)

        row_slot = 4 * x + yl
        y_two = (y + 2 + 4 * (x % 2)) % 8

        def iteration(it, _):
            logsum_pass(scores_t, pot[...], shift, row_s.at[it])
            for dx in (2, 1, 3, 0):
                for ty in (y_two, (y + 1) % 8, (y + 7) % 8, y):
                    if dx or ty is not y:
                        target = device((x + dx) % 4, ty, z, 1)
                        send(row_s.at[it], row_r.at[it, row_slot], row_send.at[it], row_recv.at[it], target)
            row_r[it, row_slot] = row_s[it]

            @pl.when(it == 0)
            def _():
                weighted = stack4(fold3(jnp.dot(split3(two), tgt_all[...], preferred_element_type=f32)))
                for n in range(8):
                    rows = pl.ds(n * 128, 128)
                    scores[rows, :] = jnp.dot(src_t[rows, :], weighted, preferred_element_type=f32)

            settle(row_r.at[it, pl.ds(0, 15)], row_recv.at[it])
            row_pot = potentials(row_r[it], log_src, log_cols)
            pot[...] = row_pot

            @pl.when(it == last)
            def _():
                fin_s[...] = row_pot
                send(fin_s, pot, fin_send.at[1], fin_recv.at[1], partner)

            logsum_pass(scores, row_pot, shift, col_s.at[it])
            for dz in FAR_8:
                send(col_s.at[it], col_r.at[it, z], col_send.at[it], col_recv.at[it], device(x, y, (z + dz) % 8, 1))
            col_r[it, z] = col_s[it]

            @pl.when(it == last)
            def _():
                for dz in (*FAR_8, 0):
                    target = device(x, y, (z + dz) % 8, 0)
                    send(col_s.at[it], col_r.at[it, z], fin_send.at[2], col_recv.at[it], target)
                row_ref[...] = jnp.where(yh == 0, row_pot[:4], row_pot[4:]) * LN2
                for n in range(4):
                    to = pl.ds(n * 128, 128)
                    rows = pl.ds(pl.multiple_of(yh * BLK + n * 128, 128), 128)
                    moved = shift[rows, :]
                    for j in range(4):
                        sum_ref[to, pl.ds(j * 128, 128)] = scores[rows, pl.ds(BLK + j * 128, 128)] + moved

            settle(col_r.at[it, pl.ds(0, 7)], col_recv.at[it])
            pot[...] = potentials(col_r[it], log_tgt, log_rows)
            return 0

        lax.fori_loop(0, ITERS, iteration, 0)
        col_ref[...] = pot[pl.ds(4, 4), :]

        settle(m0_r.at[pl.ds(0, 3)], m_send.at[0])
        settle(m1_r.at[pl.ds(0, 7)], m_send.at[1])
        settle(m2_r.at[pl.ds(0, 7)], m_send.at[2])
        settle(nrm, fin_send.at[0])
        settle(fin_s, fin_send.at[1])
        settle(col_r.at[last], fin_send.at[2])
        for it in range(ITERS):
            settle(row_r.at[it, pl.ds(0, 15)], row_send.at[it])
            settle(col_r.at[it, pl.ds(0, 7)], col_send.at[it])

    @pl.when(on_one & edge)
    def _():
        for far in range(1, 3):
            settle(src_f.at[0, rows56], swap_send.at[2 * far - 2])
            settle(smass.at[0], swap_send.at[2 * far - 1])


def finish(sum_ref, row_in, col_in, out_hbm, row_ref, col_ref, tile, sem):
    copies = []
    for n in range(8):
        rows = pl.ds(n * 64, 64)
        for j in range(4):
            lanes = pl.ds(j * 128, 128)
            tile[rows, lanes] = (sum_ref[rows, lanes] + col_in[pl.ds(j, 1), :]) * LN2
        copies.append(pltpu.make_async_copy(tile.at[rows], out_hbm.at[rows], sem.at[n]))
        copies[-1].start()
    row_ref[...] = row_in[...]
    col_ref[...] = col_in[...] * LN2
    for copy in copies:
        copy.wait()


def shards(coupling, src_pcs, tgt_pcs, src_mass, tgt_mass):
    total_rows = coupling.shape[0] * lax.axis_size("src")
    total_cols = coupling.shape[1] * lax.axis_size("tgt")
    dma = pltpu.SemaphoreType.DMA
    full, vec = jax.ShapeDtypeStruct((BLK, BLK), f32), jax.ShapeDtypeStruct((4, 128), f32)
    in_vmem, anywhere = pl.BlockSpec(memory_space=pltpu.VMEM), pl.BlockSpec(memory_space=pl.ANY)
    tile = lambda *lead: pltpu.VMEM((*lead, 8, 128), f32)
    gram = lambda *lead: pltpu.VMEM((*lead, 32, 128), f32)
    sums, row, col = pl.pallas_call(
        functools.partial(kernel, total_rows, total_cols),
        out_shape=(pltpu.VMEM((BLK, BLK), f32), pltpu.VMEM((4, 128), f32), pltpu.VMEM((4, 128), f32)),
        in_specs=[anywhere] * 5,
        out_specs=[in_vmem] * 3,
        scratch_shapes=[
            pltpu.VMEM((BLK, BLK), bf16),
            pltpu.VMEM((PCS, BLK), bf16),
            pltpu.VMEM((PCS, BLK), bf16),
            pltpu.VMEM((PAD, BLK), bf16),
            pltpu.VMEM((2 * PAD, BLK), bf16),
            pltpu.VMEM((2, PAD, BLK), f32),
            pltpu.VMEM((2, PAD, BLK), f32),
            pltpu.VMEM((2, 4, 128), f32),
            pltpu.VMEM((2, 4, 128), f32),
            pltpu.VMEM((TWO, 4 * PAD), bf16),
            pltpu.VMEM((TWO, 4 * PAD), bf16),
            pltpu.VMEM((PAD, TWO), bf16),
            pltpu.VMEM((2 * PAD, TWO), bf16),
            pltpu.VMEM((TWO, TWO), f32),
            pltpu.VMEM((TWO, TWO), f32),
            pltpu.VMEM((TWO, 128), f32),
            tile(),
            gram(),
            gram(8),
            gram(),
            gram(8),
            gram(),
            gram(8),
            gram(),
            tile(ITERS),
            tile(ITERS, 16),
            tile(ITERS),
            tile(ITERS, 8),
            tile(),
            dma((5,)),
            dma((4,)),
            dma((4,)),
            dma((3,)),
            dma((3,)),
            dma((ITERS,)),
            dma((ITERS,)),
            dma((ITERS,)),
            dma((ITERS,)),
            dma((3,)),
            dma((3,)),
        ],
        compiler_params=pltpu.CompilerParams(collective_id=0, has_side_effects=True),
        name="coupling_step",
    )(coupling, src_pcs, tgt_pcs, src_mass.reshape(4, 128), tgt_mass.reshape(4, 128))
    out, row, col = pl.pallas_call(
        finish,
        out_shape=(full, vec, vec),
        in_specs=[in_vmem] * 3,
        out_specs=[anywhere, in_vmem, in_vmem],
        scratch_shapes=[pltpu.VMEM((BLK, BLK), f32), dma((8,))],
        compiler_params=pltpu.CompilerParams(vmem_limit_bytes=8 << 20),
        name="finish",
    )(*(pltpu.with_memory_space_constraint(v, pltpu.VMEM) for v in (sums, row, col)))
    return out, row.reshape(-1), col.reshape(-1)


def solution(mesh):
    in_specs = (P("src", "tgt"), P(None, "src"), P(None, "tgt"), P("src"), P("tgt"))
    out_specs = (P("src", "tgt"), P("src"), P("tgt"))
    return jax.shard_map(shards, mesh=mesh, in_specs=in_specs, out_specs=out_specs, check_vma=False)
```

```python
import functools
import math

import jax
import jax.numpy as jnp
from jax import lax
from jax.experimental import pallas as pl
from jax.experimental.pallas import tpu as pltpu
from jax.sharding import PartitionSpec as P

PCS = 50
ITERS = 4
eps_reg = 0.5
marg_power = 1.0 / (1.0 + eps_reg)
tiny_eps = 1e-06
LN2 = math.log(2.0)
LOG2E = 1.0 / LN2

PAD = 64
SENT = 56
BLK = 512
TWO = 2 * BLK
MESH = pl.DeviceIdType.MESH
f32, bf16 = jnp.float32, jnp.bfloat16
FAR_X, FAR_8 = (2, 1, 3), (4, 3, 5, 2, 6, 1, 7)


def coords():
    s, t = lax.axis_index("src"), lax.axis_index("tgt")
    return t // 8, (s % 2) * 4 + (t // 2) % 4, s // 2, t % 2


def device(x, y, z, c):
    return (z * 2 + y // 4, (x * 4 + y % 4) * 2 + c)


def split3(v):
    hi = v.astype(bf16)
    rest = v - hi.astype(f32)
    mid = rest.astype(bf16)
    lo = (rest - mid.astype(f32)).astype(bf16)
    return jnp.concatenate([hi, mid, lo], axis=0)


def fold3(v):
    n = v.shape[0] // 3
    return (v[:n] + v[n : 2 * n]) + v[2 * n :]


def thrice(v):
    return jnp.concatenate([v, v, v, jnp.zeros_like(v)], axis=0).T.astype(bf16)


def stack4(v):
    terms = split3(v)
    return jnp.concatenate([terms, jnp.zeros((PAD, v.shape[1]), bf16)], axis=0)


def turn(pot):
    return jnp.concatenate([pot, jnp.zeros((120, 128), f32)], axis=0).T


def join(top, total, v):
    high = jnp.maximum(top, jnp.max(v, axis=0))
    return high, total * jnp.exp2(top - high) + jnp.sum(jnp.exp2(v - high[None]), axis=0)


def over_rows(tops, sums):
    top = jnp.max(tops, axis=0, keepdims=True)
    return top + jnp.log2(jnp.sum(sums * jnp.exp2(tops - top), axis=0, keepdims=True))


def logsum_pass(table, pot, shift, out):
    turned = turn(pot)
    for pair in range(4):
        tops = [jnp.full((8, 128), -1e30, f32)] * 2
        sums = [jnp.zeros((8, 128), f32)] * 2
        for p in range(8):
            rows = pl.ds(p * 128, 128)
            if pair == 0:
                moved = jnp.broadcast_to(turned[:, p : p + 1], (128, 128))
                shift[rows, :] = moved
            else:
                moved = shift[rows, :]
            moved = moved.reshape(16, 8, 128)
            for k in range(2):
                j = 2 * pair + k
                v = table[rows, j * 128 : (j + 1) * 128].reshape(16, 8, 128) + moved
                tops[k], sums[k] = join(tops[k], sums[k], v)
        for k in range(2):
            out[pl.ds(2 * pair + k, 1), :] = over_rows(tops[k], sums[k])


def potentials(v, log_mass, log_count):
    top = jnp.max(v, axis=0)
    total = top + jnp.log2(jnp.sum(jnp.exp2(v - top[None]), axis=0))
    return marg_power * (log_mass - (total - log_count))


def send(src, dst, send_sem, recv_sem, target):
    pltpu.make_async_remote_copy(
        src_ref=src, dst_ref=dst, send_sem=send_sem, recv_sem=recv_sem,
        device_id=target, device_id_type=MESH,
    ).start()


def settle(ref, sem):
    pltpu.make_async_copy(ref, ref, sem).wait()


def greet(targets):
    barrier = pltpu.get_barrier_semaphore()
    for target in targets:
        pl.semaphore_signal(barrier, inc=1, device_id=target, device_id_type=MESH)


def kernel(
    total_rows, total_cols,
    coupling_hbm, src_hbm, tgt_hbm, smass_hbm, tmass_hbm,
    sum_ref, row_ref, col_ref,
    coupling, src_in, tgt_in, src_b, tgt_two, src_f, tgt_f, smass, tmass,
    src_t, tgt_t, src_all, tgt_all, scores, scores_t, shift, pot,
    m0_s, m0_r, m1_s, m1_r, m2_s, m2_r, nrm, row_s, row_r, col_s, col_r, fin_s,
    load_sem, swap_send, swap_recv, m_send, m_recv, row_send, row_recv, col_send, col_recv, fin_send, fin_recv,
):
    x, y, z, c = coords()
    yh, yl = y // 4, y % 4
    on_one, on_zero = c == 1, c == 0

    loads = [
        pltpu.make_async_copy(src_hbm, src_in, load_sem.at[0]),
        pltpu.make_async_copy(tgt_hbm, tgt_in, load_sem.at[1]),
        pltpu.make_async_copy(coupling_hbm, coupling, load_sem.at[2]),
        pltpu.make_async_copy(smass_hbm, smass.at[yh], load_sem.at[3]),
        pltpu.make_async_copy(tmass_hbm, tmass.at[c], load_sem.at[4]),
    ]
    for copy in loads:
        copy.start()

    row_peers = [(dx, dy) for dx in (2, 1, 3, 0) for dy in (2, 6, 1, 7)]
    ones = [device((x + dx) % 4, (y + dy) % 8, z, 1) for dx, dy in row_peers]
    ones += [device((x + dx) % 4, y, z, 1) for dx in FAR_X]
    ones += [device(x, (y + dy) % 8, z, 1) for dy in (4, 3, 5)]
    ones += [device(x, y, (z + dz) % 8, 1) for dz in FAR_8]
    near = [device((x + dx) % 4, y, z, 0) for dx in (2, 1, 3, 0)]

    @pl.when(on_one)
    def _():
        greet(ones + near)

    @pl.when(on_zero)
    def _():
        greet([device(x, y, (z + dz) % 8, 1) for dz in FAR_8])
        greet([device((x + dx) % 4, y, z, 1) for dx in (2, 1, 3, 0)])

    src_b[pl.ds(48, 16), :] = jnp.zeros((16, BLK), bf16)
    tgt_two[pl.ds(48, 16), :] = jnp.zeros((16, BLK), bf16)
    tgt_two[pl.ds(112, 16), :] = jnp.zeros((16, BLK), bf16)
    for copy in loads[:2]:
        copy.wait()
    src_b[pl.ds(0, PCS), :] = src_in[...]
    tgt_two[pl.ds(0, PCS), :] = tgt_in[...]
    tgt_two[pl.ds(PAD, PCS), :] = tgt_in[...]
    loads[2].wait()

    panel = jnp.dot(src_b[...], coupling[...], preferred_element_type=f32)
    wide = fold3(
        lax.dot_general(
            split3(panel), tgt_two[...], (((1,), (1,)), ((), ())), preferred_element_type=f32
        )
    )
    left = lax.broadcasted_iota(jnp.int32, (32, 128), 1) < PAD
    packed = jnp.where(left, wide[:32], wide[32:])
    m0_s[...] = packed

    barrier = pltpu.get_barrier_semaphore()
    own0 = 2 * x + c

    @pl.when(on_one)
    def _():
        pl.semaphore_wait(barrier, len(ones) + 7 + 4)
        m0_r[own0] = packed
        for dx in FAR_X:
            send(m0_s, m0_r.at[own0], m_send.at[0], m_recv.at[0], device((x + dx) % 4, y, z, 1))

    @pl.when(on_zero)
    def _():
        pl.semaphore_wait(barrier, 4)
        for dx in (2, 1, 3, 0):
            send(m0_s, m0_r.at[own0], m_send.at[0], m_recv.at[0], device((x + dx) % 4, y, z, 1))

    for ref, own, block in ((src_f, yh, src_b), (tgt_f, c, tgt_two)):
        for side in range(2):
            ref[side, pl.ds(SENT, 8), :] = jnp.zeros((8, BLK), f32)
        ref[own, pl.ds(0, SENT), :] = block[pl.ds(0, PAD), :].astype(f32)[:SENT]
    for copy in loads[3:]:
        copy.wait()

    rows56 = pl.ds(0, SENT)

    def moment_of(packed_sum):
        return packed_sum * (total_rows * total_cols) ** (-0.5)

    def factor_of(packed_sum):
        moment = moment_of(packed_sum)
        square = jnp.sum(moment * moment, axis=0, keepdims=True)
        square = jnp.sum(square, axis=1, keepdims=True) * (1.0 / (PCS * PCS))
        return (2.0 / (eps_reg * PCS) * LOG2E) / jnp.sqrt(square + tiny_eps)

    def packed_two(v):
        return jnp.concatenate([jnp.where(left, v, 0.0), jnp.where(left, 0.0, v)], axis=0)

    log_rows, log_cols = math.log2(total_rows), math.log2(total_cols)
    partner = device(x, y, z, 1 - c)
    last = ITERS - 1

    @pl.when(on_zero)
    def _():
        send(tgt_f.at[0, rows56], tgt_f.at[0, rows56], swap_send.at[0], swap_recv.at[0], partner)
        send(tmass.at[0], tmass.at[0], swap_send.at[1], swap_recv.at[1], partner)
        src_t[pl.ds(0, BLK), :] = thrice(src_f[yh])
        log_tgt = jnp.log2(tmass[0])

        settle(nrm, fin_recv.at[0])
        two = packed_two(moment_of(nrm[...]))
        raw = fold3(jnp.dot(split3(two), tgt_two[...], preferred_element_type=f32))
        sum_ref[...] = jnp.dot(
            src_t[pl.ds(0, BLK), :], stack4(raw * factor_of(nrm[...])), preferred_element_type=f32
        )

        settle(pot, fin_recv.at[1])
        half = jnp.where(yh == 0, pot[pl.ds(0, 4), :], pot[pl.ds(4, 4), :])
        row_ref[...] = half * LN2
        turned = turn(jnp.concatenate([half, jnp.zeros((4, 128), f32)], axis=0))
        for p in range(4):
            rows = pl.ds(p * 128, 128)
            moved = jnp.broadcast_to(turned[:, p : p + 1], (128, 128))
            for j in range(4):
                lanes = pl.ds(j * 128, 128)
                sum_ref[rows, lanes] = sum_ref[rows, lanes] + moved

        settle(col_r.at[last], col_recv.at[last])
        col_ref[...] = potentials(col_r[last][:, :4, :], log_tgt, log_rows)

        settle(m0_r.at[pl.ds(0, 4)], m_send.at[0])
        settle(tgt_f.at[0, rows56], swap_send.at[0])
        settle(tmass.at[0], swap_send.at[1])

    edge = (yl == 0) | (yl == 3)

    @pl.when(on_one & edge)
    def _():
        way = jnp.where(yl == 3, 1, 7)
        for far in range(1, 3):
            target = device(x, (y + far * way) % 8, z, 1)
            send(src_f.at[yh, rows56], src_f.at[yh, rows56], swap_send.at[2 * far - 2], swap_recv.at[2], target)
            send(smass.at[yh], smass.at[yh], swap_send.at[2 * far - 1], swap_recv.at[3], target)

    @pl.when(on_one)
    def _():
        tgt_t[pl.ds(BLK, BLK), :] = thrice(tgt_f[1])

        settle(m0_r.at[pl.ds(0, 7)], m_recv.at[0])
        part = jnp.sum(m0_r[...], axis=0)
        m1_s[...] = part
        for dy in FAR_8:
            send(m1_s, m1_r.at[y], m_send.at[1], m_recv.at[1], device(x, (y + dy) % 8, z, 1))
        m1_r[y] = part

        settle(tgt_f.at[0, rows56], swap_recv.at[0])
        settle(tmass.at[0], swap_recv.at[1])
        tgt_t[pl.ds(0, BLK), :] = thrice(tgt_f[0])
        near_b = tgt_f[0].astype(bf16)
        tgt_all[pl.ds(0, PAD), pl.ds(0, BLK)] = near_b
        tgt_all[pl.ds(PAD, PAD), pl.ds(0, BLK)] = near_b
        tgt_all[:, pl.ds(BLK, BLK)] = tgt_two[...]

        settle(m1_r.at[pl.ds(0, 7)], m_recv.at[1])
        part = jnp.sum(m1_r[...], axis=0)
        m2_s[...] = part
        for dz in FAR_8:
            send(m2_s, m2_r.at[z], m_send.at[2], m_recv.at[2], device(x, y, (z + dz) % 8, 1))
        m2_r[z] = part

        settle(src_f.at[0, rows56], swap_recv.at[2])
        settle(smass.at[0], swap_recv.at[3])
        for side in range(2):
            src_t[pl.ds(side * BLK, BLK), :] = thrice(src_f[side])
            src_all[:, pl.ds(side * BLK, BLK)] = src_f[side].astype(bf16)
        log_src = jnp.log2(jnp.concatenate([smass[0], smass[1]], axis=0))
        log_tgt = jnp.log2(jnp.concatenate([tmass[0], tmass[1]], axis=0))

        settle(m2_r.at[pl.ds(0, 7)], m_recv.at[2])
        total = jnp.sum(m2_r[...], axis=0)
        nrm[...] = total
        send(nrm, nrm, fin_send.at[0], fin_recv.at[0], partner)

        turned = jnp.concatenate([packed_two(moment_of(total)), jnp.zeros((PAD, 128), f32)], axis=0).T
        back = turned[:PAD, :PAD] + turned[PAD:, :PAD]
        factor = factor_of(total)
        raw = fold3(jnp.dot(split3(back), src_all[...], preferred_element_type=f32))
        weighted_t = stack4(raw * factor)
        tops = [jnp.full((8, 128), -1e30, f32)] * 8
        sums = [jnp.zeros((8, 128), f32)] * 8
        for n in range(9):
            if n < 8:
                rows = pl.ds(n * 128, 128)
                scores_t[rows, :] = jnp.dot(tgt_t[rows, :], weighted_t, preferred_element_type=f32)
            if n:
                rows = pl.ds((n - 1) * 128, 128)
                for j in range(8):
                    v = scores_t[rows, j * 128 : (j + 1) * 128].reshape(16, 8, 128)
                    tops[j], sums[j] = join(tops[j], sums[j], v)
        for j in range(8):
            row_s[0, pl.ds(j, 1), :] = over_rows(tops[j], sums[j])

        row_slot = 4 * x + yl
        y_two = (y + 2 + 4 * (x % 2)) % 8

        def iteration(it, _):
            for dx in (2, 1, 3, 0):
                for ty in (y_two, (y + 1) % 8, (y + 7) % 8, y):
                    if dx or ty is not y:
                        target = device((x + dx) % 4, ty, z, 1)
                        send(row_s.at[it], row_r.at[it, row_slot], row_send.at[it], row_recv.at[it], target)
            row_r[it, row_slot] = row_s[it]

            @pl.when(it == 0)
            def _():
                two = packed_two(moment_of(nrm[...]))
                raw = fold3(jnp.dot(split3(two), tgt_all[...], preferred_element_type=f32))
                weighted = stack4(raw * factor_of(nrm[...]))
                for n in range(8):
                    rows = pl.ds(n * 128, 128)
                    scores[rows, :] = jnp.dot(src_t[rows, :], weighted, preferred_element_type=f32)

            settle(row_r.at[it, pl.ds(0, 15)], row_recv.at[it])
            row_pot = potentials(row_r[it], log_src, log_cols)
            pot[...] = row_pot

            @pl.when(it == last)
            def _():
                fin_s[...] = row_pot
                send(fin_s, pot, fin_send.at[1], fin_recv.at[1], partner)

            logsum_pass(scores, row_pot, shift, col_s.at[it])
            for dz in FAR_8:
                send(col_s.at[it], col_r.at[it, z], col_send.at[it], col_recv.at[it], device(x, y, (z + dz) % 8, 1))
            col_r[it, z] = col_s[it]

            @pl.when(it == last)
            def _():
                for dz in (*FAR_8, 0):
                    target = device(x, y, (z + dz) % 8, 0)
                    send(col_s.at[it], col_r.at[it, z], fin_send.at[2], col_recv.at[it], target)
                row_ref[...] = jnp.where(yh == 0, row_pot[:4], row_pot[4:]) * LN2
                for n in range(4):
                    to = pl.ds(n * 128, 128)
                    rows = pl.ds(pl.multiple_of(yh * BLK + n * 128, 128), 128)
                    moved = shift[rows, :]
                    for j in range(4):
                        sum_ref[to, pl.ds(j * 128, 128)] = scores[rows, pl.ds(BLK + j * 128, 128)] + moved

            settle(col_r.at[it, pl.ds(0, 7)], col_recv.at[it])
            pot[...] = potentials(col_r[it], log_tgt, log_rows)

            @pl.when(it < last)
            def _():
                logsum_pass(scores_t, pot[...], shift, row_s.at[it + 1])

            return 0

        lax.fori_loop(0, ITERS, iteration, 0)
        col_ref[...] = pot[pl.ds(4, 4), :]

        settle(m0_r.at[pl.ds(0, 3)], m_send.at[0])
        settle(m1_r.at[pl.ds(0, 7)], m_send.at[1])
        settle(m2_r.at[pl.ds(0, 7)], m_send.at[2])
        settle(nrm, fin_send.at[0])
        settle(fin_s, fin_send.at[1])
        settle(col_r.at[last], fin_send.at[2])
        for it in range(ITERS):
            settle(row_r.at[it, pl.ds(0, 15)], row_send.at[it])
            settle(col_r.at[it, pl.ds(0, 7)], col_send.at[it])

    @pl.when(on_one & edge)
    def _():
        for far in range(1, 3):
            settle(src_f.at[0, rows56], swap_send.at[2 * far - 2])
            settle(smass.at[0], swap_send.at[2 * far - 1])


def finish(sum_ref, row_in, col_in, out_hbm, row_ref, col_ref, tile, sem):
    copies = []
    for n in range(8):
        rows = pl.ds(n * 64, 64)
        for j in range(4):
            lanes = pl.ds(j * 128, 128)
            tile[rows, lanes] = (sum_ref[rows, lanes] + col_in[pl.ds(j, 1), :]) * LN2
        copies.append(pltpu.make_async_copy(tile.at[rows], out_hbm.at[rows], sem.at[n]))
        copies[-1].start()
    row_ref[...] = row_in[...]
    col_ref[...] = col_in[...] * LN2
    for copy in copies:
        copy.wait()


def shards(coupling, src_pcs, tgt_pcs, src_mass, tgt_mass):
    total_rows = coupling.shape[0] * lax.axis_size("src")
    total_cols = coupling.shape[1] * lax.axis_size("tgt")
    dma = pltpu.SemaphoreType.DMA
    full, vec = jax.ShapeDtypeStruct((BLK, BLK), f32), jax.ShapeDtypeStruct((4, 128), f32)
    in_vmem, anywhere = pl.BlockSpec(memory_space=pltpu.VMEM), pl.BlockSpec(memory_space=pl.ANY)
    tile = lambda *lead: pltpu.VMEM((*lead, 8, 128), f32)
    gram = lambda *lead: pltpu.VMEM((*lead, 32, 128), f32)
    sums, row, col = pl.pallas_call(
        functools.partial(kernel, total_rows, total_cols),
        out_shape=(pltpu.VMEM((BLK, BLK), f32), pltpu.VMEM((4, 128), f32), pltpu.VMEM((4, 128), f32)),
        in_specs=[anywhere] * 5,
        out_specs=[in_vmem] * 3,
        scratch_shapes=[
            pltpu.VMEM((BLK, BLK), bf16),
            pltpu.VMEM((PCS, BLK), bf16),
            pltpu.VMEM((PCS, BLK), bf16),
            pltpu.VMEM((PAD, BLK), bf16),
            pltpu.VMEM((2 * PAD, BLK), bf16),
            pltpu.VMEM((2, PAD, BLK), f32),
            pltpu.VMEM((2, PAD, BLK), f32),
            pltpu.VMEM((2, 4, 128), f32),
            pltpu.VMEM((2, 4, 128), f32),
            pltpu.VMEM((TWO, 4 * PAD), bf16),
            pltpu.VMEM((TWO, 4 * PAD), bf16),
            pltpu.VMEM((PAD, TWO), bf16),
            pltpu.VMEM((2 * PAD, TWO), bf16),
            pltpu.VMEM((TWO, TWO), f32),
            pltpu.VMEM((TWO, TWO), f32),
            pltpu.VMEM((TWO, 128), f32),
            tile(),
            gram(),
            gram(8),
            gram(),
            gram(8),
            gram(),
            gram(8),
            gram(),
            tile(ITERS),
            tile(ITERS, 16),
            tile(ITERS),
            tile(ITERS, 8),
            tile(),
            dma((5,)),
            dma((4,)),
            dma((4,)),
            dma((3,)),
            dma((3,)),
            dma((ITERS,)),
            dma((ITERS,)),
            dma((ITERS,)),
            dma((ITERS,)),
            dma((3,)),
            dma((3,)),
        ],
        compiler_params=pltpu.CompilerParams(collective_id=0, has_side_effects=True),
        name="coupling_step",
    )(coupling, src_pcs, tgt_pcs, src_mass.reshape(4, 128), tgt_mass.reshape(4, 128))
    out, row, col = pl.pallas_call(
        finish,
        out_shape=(full, vec, vec),
        in_specs=[in_vmem] * 3,
        out_specs=[anywhere, in_vmem, in_vmem],
        scratch_shapes=[pltpu.VMEM((BLK, BLK), f32), dma((8,))],
        compiler_params=pltpu.CompilerParams(vmem_limit_bytes=8 << 20),
        name="finish",
    )(*(pltpu.with_memory_space_constraint(v, pltpu.VMEM) for v in (sums, row, col)))
    return out, row.reshape(-1), col.reshape(-1)


def solution(mesh):
    in_specs = (P("src", "tgt"), P(None, "src"), P(None, "tgt"), P("src"), P("tgt"))
    out_specs = (P("src", "tgt"), P("src"), P("tgt"))
    return jax.shard_map(shards, mesh=mesh, in_specs=in_specs, out_specs=out_specs, check_vma=False)
```

```python
import functools
import math

import jax
import jax.numpy as jnp
from jax import lax
from jax.experimental import pallas as pl
from jax.experimental.pallas import tpu as pltpu
from jax.sharding import PartitionSpec as P

PCS = 50
ITERS = 4
eps_reg = 0.5
marg_power = 1.0 / (1.0 + eps_reg)
tiny_eps = 1e-06
LN2 = math.log(2.0)
LOG2E = 1.0 / LN2

PAD = 64
SENT = 56
BLK = 512
TWO = 2 * BLK
MESH = pl.DeviceIdType.MESH
f32, bf16 = jnp.float32, jnp.bfloat16
FAR_X, FAR_8 = (2, 1, 3), (4, 3, 5, 2, 6, 1, 7)


def hops(d):
    return min(d[0], 4 - d[0]) + min(d[1], 8 - d[1])


NEAR = sorted(
    (
        min(((dx, dy), ((dx + 2) % 4, dy + 4)), key=lambda d: (hops(d), (d[0] + d[1]) % 2, d))
        for dx in range(4)
        for dy in range(4)
    ),
    key=hops,
    reverse=True,
)[:-1]


def coords():
    s, t = lax.axis_index("src"), lax.axis_index("tgt")
    return t // 8, (s % 2) * 4 + (t // 2) % 4, s // 2, t % 2


def device(x, y, z, c):
    return (z * 2 + y // 4, (x * 4 + y % 4) * 2 + c)


def split3(v):
    hi = v.astype(bf16)
    rest = v - hi.astype(f32)
    mid = rest.astype(bf16)
    lo = (rest - mid.astype(f32)).astype(bf16)
    return jnp.concatenate([hi, mid, lo], axis=0)


def fold3(v):
    n = v.shape[0] // 3
    return (v[:n] + v[n : 2 * n]) + v[2 * n :]


def thrice(v):
    return jnp.concatenate([v, v, v, jnp.zeros_like(v)], axis=0).T.astype(bf16)


def stack4(v):
    terms = split3(v)
    return jnp.concatenate([terms, jnp.zeros((PAD, v.shape[1]), bf16)], axis=0)


def turn(pot):
    return jnp.concatenate([pot, jnp.zeros((120, 128), f32)], axis=0).T


def join(top, total, v):
    high = jnp.maximum(top, jnp.max(v, axis=0))
    return high, total * jnp.exp2(top - high) + jnp.sum(jnp.exp2(v - high[None]), axis=0)


def over_rows(tops, sums):
    top = jnp.max(tops, axis=0, keepdims=True)
    return top + jnp.log2(jnp.sum(sums * jnp.exp2(tops - top), axis=0, keepdims=True))


def logsum_pass(table, pot, shift, out):
    turned = turn(pot)
    for pair in range(4):
        tops = [jnp.full((8, 128), -1e30, f32)] * 2
        sums = [jnp.zeros((8, 128), f32)] * 2
        for p in range(8):
            rows = pl.ds(p * 128, 128)
            if pair == 0:
                moved = jnp.broadcast_to(turned[:, p : p + 1], (128, 128))
                shift[rows, :] = moved
            else:
                moved = shift[rows, :]
            moved = moved.reshape(16, 8, 128)
            for k in range(2):
                j = 2 * pair + k
                v = table[rows, j * 128 : (j + 1) * 128].reshape(16, 8, 128) + moved
                tops[k], sums[k] = join(tops[k], sums[k], v)
        for k in range(2):
            out[pl.ds(2 * pair + k, 1), :] = over_rows(tops[k], sums[k])


def potentials(v, log_mass, log_count):
    top = jnp.max(v, axis=0)
    total = top + jnp.log2(jnp.sum(jnp.exp2(v - top[None]), axis=0))
    return marg_power * (log_mass - (total - log_count))


def send(src, dst, send_sem, recv_sem, target):
    pltpu.make_async_remote_copy(
        src_ref=src, dst_ref=dst, send_sem=send_sem, recv_sem=recv_sem,
        device_id=target, device_id_type=MESH,
    ).start()


def settle(ref, sem):
    pltpu.make_async_copy(ref, ref, sem).wait()


def greet(targets):
    barrier = pltpu.get_barrier_semaphore()
    for target in targets:
        pl.semaphore_signal(barrier, inc=1, device_id=target, device_id_type=MESH)


def kernel(
    total_rows, total_cols,
    coupling_hbm, src_hbm, tgt_hbm, smass_hbm, tmass_hbm,
    sum_ref, row_ref, col_ref,
    coupling, src_in, tgt_in, src_b, tgt_two, src_f, tgt_f, tgt_k, smass, tmass, tmass_k,
    src_t, tgt_t, src_all, tgt_all, tgt_own, scores, scores_t, shift, pot,
    m0_s, m0_r, m1_s, m1_r, m2_s, m2_r, nrm, row_s, row_r, col_s, col_r, fin_s,
    load_sem, swap_send, swap_recv, take_send, take_recv, m_send, m_recv, row_send, row_recv, col_send, col_recv, fin_send, fin_recv,
):
    x, y, z, c = coords()
    yh, yl = y // 4, y % 4
    on_one, on_zero = c == 1, c == 0

    loads = [
        pltpu.make_async_copy(src_hbm, src_in, load_sem.at[0]),
        pltpu.make_async_copy(tgt_hbm, tgt_in, load_sem.at[1]),
        pltpu.make_async_copy(coupling_hbm, coupling, load_sem.at[2]),
        pltpu.make_async_copy(smass_hbm, smass.at[yh], load_sem.at[3]),
        pltpu.make_async_copy(tmass_hbm, tmass.at[c], load_sem.at[4]),
    ]
    for copy in loads:
        copy.start()

    plane = sorted({*NEAR, *((dx, 0) for dx in FAR_X), *((0, dy) for dy in FAR_8)}, key=hops, reverse=True)
    ones = [device((x + dx) % 4, (y + dy) % 8, z, 1) for dx, dy in plane]
    ones += [device(x, y, (z + dz) % 8, 1) for dz in FAR_8]
    near = [device((x + dx) % 4, y, z, 0) for dx in (2, 1, 3, 0)]

    @pl.when(on_one)
    def _():
        greet(ones + near)

    @pl.when(on_zero)
    def _():
        greet([device(x, y, (z + dz) % 8, 1) for dz in FAR_8])
        greet([device((x + dx) % 4, y, z, 1) for dx in (2, 1, 3, 0)])

    src_b[pl.ds(48, 16), :] = jnp.zeros((16, BLK), bf16)
    tgt_two[pl.ds(48, 16), :] = jnp.zeros((16, BLK), bf16)
    tgt_two[pl.ds(112, 16), :] = jnp.zeros((16, BLK), bf16)
    for copy in loads[:2]:
        copy.wait()
    src_b[pl.ds(0, PCS), :] = src_in[...]
    tgt_two[pl.ds(0, PCS), :] = tgt_in[...]
    tgt_two[pl.ds(PAD, PCS), :] = tgt_in[...]
    loads[2].wait()

    panel = jnp.dot(src_b[...], coupling[...], preferred_element_type=f32)
    wide = fold3(
        lax.dot_general(
            split3(panel), tgt_two[...], (((1,), (1,)), ((), ())), preferred_element_type=f32
        )
    )
    left = lax.broadcasted_iota(jnp.int32, (32, 128), 1) < PAD
    packed = jnp.where(left, wide[:32], wide[32:])
    m0_s[...] = packed

    barrier = pltpu.get_barrier_semaphore()
    own0 = 2 * x + c

    @pl.when(on_one)
    def _():
        pl.semaphore_wait(barrier, len(ones) + 7 + 4)
        m0_r[own0] = packed
        for dx in FAR_X:
            send(m0_s, m0_r.at[own0], m_send.at[0], m_recv.at[0], device((x + dx) % 4, y, z, 1))

    @pl.when(on_zero)
    def _():
        pl.semaphore_wait(barrier, 4)
        for dx in (2, 1, 3, 0):
            send(m0_s, m0_r.at[own0], m_send.at[0], m_recv.at[0], device((x + dx) % 4, y, z, 1))

    for side in range(2):
        tgt_k[side, pl.ds(SENT, 8), :] = jnp.zeros((8, BLK), f32)
    for ref, own, block in ((src_f, yh, src_b), (tgt_f, c, tgt_two)):
        for side in range(2):
            ref[side, pl.ds(SENT, 8), :] = jnp.zeros((8, BLK), f32)
        ref[own, pl.ds(0, SENT), :] = block[pl.ds(0, PAD), :].astype(f32)[:SENT]
    for copy in loads[3:]:
        copy.wait()

    rows56 = pl.ds(0, SENT)

    def moment_of(packed_sum):
        return packed_sum * (total_rows * total_cols) ** (-0.5)

    def factor_of(packed_sum):
        moment = moment_of(packed_sum)
        square = jnp.sum(moment * moment, axis=0, keepdims=True)
        square = jnp.sum(square, axis=1, keepdims=True) * (1.0 / (PCS * PCS))
        return (2.0 / (eps_reg * PCS) * LOG2E) / jnp.sqrt(square + tiny_eps)

    def packed_two(v):
        return jnp.concatenate([jnp.where(left, v, 0.0), jnp.where(left, 0.0, v)], axis=0)

    log_rows, log_cols = math.log2(total_rows), math.log2(total_cols)
    partner = device(x, y, z, 1 - c)
    last = ITERS - 1

    @pl.when(on_zero)
    def _():
        send(tgt_f.at[0, rows56], tgt_f.at[0, rows56], swap_send.at[0], swap_recv.at[0], partner)
        send(tmass.at[0], tmass.at[0], swap_send.at[1], swap_recv.at[1], partner)
        src_t[pl.ds(0, BLK), :] = thrice(src_f[yh])
        log_tgt = jnp.log2(tmass[0])

        settle(nrm, fin_recv.at[0])
        two = packed_two(moment_of(nrm[...]))
        raw = fold3(jnp.dot(split3(two), tgt_two[...], preferred_element_type=f32))
        sum_ref[...] = jnp.dot(
            src_t[pl.ds(0, BLK), :], stack4(raw * factor_of(nrm[...])), preferred_element_type=f32
        )

        settle(pot, fin_recv.at[1])
        half = jnp.where(yh == 0, pot[pl.ds(0, 4), :], pot[pl.ds(4, 4), :])
        row_ref[...] = half * LN2
        turned = turn(jnp.concatenate([half, jnp.zeros((4, 128), f32)], axis=0))
        for p in range(4):
            rows = pl.ds(p * 128, 128)
            moved = jnp.broadcast_to(turned[:, p : p + 1], (128, 128))
            for j in range(4):
                lanes = pl.ds(j * 128, 128)
                sum_ref[rows, lanes] = sum_ref[rows, lanes] + moved

        settle(col_r.at[last], col_recv.at[last])
        col_ref[...] = potentials(col_r[last][:, :4, :], log_tgt, log_rows)

        settle(m0_r.at[pl.ds(0, 4)], m_send.at[0])
        settle(tgt_f.at[0, rows56], swap_send.at[0])
        settle(tmass.at[0], swap_send.at[1])

    edge = (yl == 0) | (yl == 3)

    @pl.when(on_one & edge)
    def _():
        way = jnp.where(yl == 3, 1, 7)
        for far in range(1, 3):
            target = device(x, (y + far * way) % 8, z, 1)
            send(src_f.at[yh, rows56], src_f.at[yh, rows56], swap_send.at[2 * far - 2], swap_recv.at[2], target)
            send(smass.at[yh], smass.at[yh], swap_send.at[2 * far - 1], swap_recv.at[3], target)

    @pl.when(on_one)
    def _():
        settle(m0_r.at[pl.ds(0, 7)], m_recv.at[0])
        part = jnp.sum(m0_r[...], axis=0)
        m1_s[...] = part
        for dy in FAR_8:
            send(m1_s, m1_r.at[y], m_send.at[1], m_recv.at[1], device(x, (y + dy) % 8, z, 1))
        m1_r[y] = part

        settle(tgt_f.at[0, rows56], swap_recv.at[0])
        settle(tmass.at[0], swap_recv.at[1])

        @pl.when(yh == 1)
        def _():
            target = device((x + 2) % 4, y, z, 1)
            for core in range(2):
                send(tgt_f.at[core, rows56], tgt_k.at[core, rows56], take_send.at[core], take_recv.at[core], target)
            send(tmass, tmass_k, take_send.at[2], take_recv.at[2], target)

        @pl.when(yh == 0)
        def _():
            for core in range(2):
                tgt_k[core, rows56, :] = tgt_f[core, rows56, :]
            tmass_k[...] = tmass[...]

        for core in range(2):
            lanes = pl.ds(core * BLK, BLK)
            block = tgt_f[core].astype(bf16)
            tgt_own[pl.ds(0, PAD), lanes] = block
            tgt_own[pl.ds(PAD, PAD), lanes] = block

        settle(m1_r.at[pl.ds(0, 7)], m_recv.at[1])
        part = jnp.sum(m1_r[...], axis=0)
        m2_s[...] = part
        for dz in FAR_8:
            send(m2_s, m2_r.at[z], m_send.at[2], m_recv.at[2], device(x, y, (z + dz) % 8, 1))
        m2_r[z] = part

        settle(src_f.at[0, rows56], swap_recv.at[2])
        settle(smass.at[0], swap_recv.at[3])
        for side in range(2):
            src_t[pl.ds(side * BLK, BLK), :] = thrice(src_f[side])
            src_all[:, pl.ds(side * BLK, BLK)] = src_f[side].astype(bf16)
        log_src = jnp.log2(jnp.concatenate([smass[0], smass[1]], axis=0))
        log_own = jnp.log2(jnp.concatenate([tmass[0], tmass[1]], axis=0))

        @pl.when(yh == 1)
        def _():
            for core in range(2):
                settle(tgt_k.at[core, rows56], take_recv.at[core])
            settle(tmass_k, take_recv.at[2])

        log_tgt = jnp.log2(jnp.concatenate([tmass_k[0], tmass_k[1]], axis=0))
        for core in range(2):
            lanes = pl.ds(core * BLK, BLK)
            tgt_t[lanes, :] = thrice(tgt_k[core])
            block = tgt_k[core].astype(bf16)
            tgt_all[pl.ds(0, PAD), lanes] = block
            tgt_all[pl.ds(PAD, PAD), lanes] = block

        settle(m2_r.at[pl.ds(0, 7)], m_recv.at[2])
        total = jnp.sum(m2_r[...], axis=0)
        nrm[...] = total
        send(nrm, nrm, fin_send.at[0], fin_recv.at[0], partner)

        turned = jnp.concatenate([packed_two(moment_of(total)), jnp.zeros((PAD, 128), f32)], axis=0).T
        back = turned[:PAD, :PAD] + turned[PAD:, :PAD]
        factor = factor_of(total)
        raw = fold3(jnp.dot(split3(back), src_all[...], preferred_element_type=f32))
        weighted_t = stack4(raw * factor)
        tops = [jnp.full((8, 128), -1e30, f32)] * 8
        sums = [jnp.zeros((8, 128), f32)] * 8
        for n in range(9):
            if n < 8:
                rows = pl.ds(n * 128, 128)
                scores_t[rows, :] = jnp.dot(tgt_t[rows, :], weighted_t, preferred_element_type=f32)
            if n:
                rows = pl.ds((n - 1) * 128, 128)
                for j in range(8):
                    v = scores_t[rows, j * 128 : (j + 1) * 128].reshape(16, 8, 128)
                    tops[j], sums[j] = join(tops[j], sums[j], v)
        for j in range(8):
            row_s[0, pl.ds(j, 1), :] = over_rows(tops[j], sums[j])

        row_slot = 4 * ((x + 2 * yh) % 4) + yl

        def score(targets):
            two = packed_two(moment_of(nrm[...]))
            raw = fold3(jnp.dot(split3(two), targets[...], preferred_element_type=f32))
            weighted = stack4(raw * factor_of(nrm[...]))
            for n in range(8):
                rows = pl.ds(n * 128, 128)
                scores[rows, :] = jnp.dot(src_t[rows, :], weighted, preferred_element_type=f32)

        def iteration(it, _):
            for dx, dy in NEAR:
                target = device((x + 4 - dx) % 4, (y + 8 - dy) % 8, z, 1)
                send(row_s.at[it], row_r.at[it, row_slot], row_send.at[it], row_recv.at[it], target)
            row_r[it, row_slot] = row_s[it]

            @pl.when(it == 0)
            def _():
                score(tgt_all)

            @pl.when(it == last)
            def _():
                score(tgt_own)

            settle(row_r.at[it, pl.ds(0, 15)], row_recv.at[it])
            row_pot = potentials(row_r[it], log_src, log_cols)
            pot[...] = row_pot

            @pl.when(it == last)
            def _():
                fin_s[...] = row_pot
                send(fin_s, pot, fin_send.at[1], fin_recv.at[1], partner)

            logsum_pass(scores, row_pot, shift, col_s.at[it])
            for dz in FAR_8:
                send(col_s.at[it], col_r.at[it, z], col_send.at[it], col_recv.at[it], device(x, y, (z + dz) % 8, 1))
            col_r[it, z] = col_s[it]

            @pl.when(it == last)
            def _():
                for dz in (*FAR_8, 0):
                    target = device(x, y, (z + dz) % 8, 0)
                    send(col_s.at[it], col_r.at[it, z], fin_send.at[2], col_recv.at[it], target)
                row_ref[...] = jnp.where(yh == 0, row_pot[:4], row_pot[4:]) * LN2
                for n in range(4):
                    to = pl.ds(n * 128, 128)
                    rows = pl.ds(pl.multiple_of(yh * BLK + n * 128, 128), 128)
                    moved = shift[rows, :]
                    for j in range(4):
                        sum_ref[to, pl.ds(j * 128, 128)] = scores[rows, pl.ds(BLK + j * 128, 128)] + moved

            settle(col_r.at[it, pl.ds(0, 7)], col_recv.at[it])
            pot[...] = potentials(col_r[it], jnp.where(it == last, log_own, log_tgt), log_rows)

            @pl.when(it < last)
            def _():
                logsum_pass(scores_t, pot[...], shift, row_s.at[it + 1])

            return 0

        lax.fori_loop(0, ITERS, iteration, 0)
        col_ref[...] = pot[pl.ds(4, 4), :]

        settle(m0_r.at[pl.ds(0, 3)], m_send.at[0])
        settle(m1_r.at[pl.ds(0, 7)], m_send.at[1])
        settle(m2_r.at[pl.ds(0, 7)], m_send.at[2])
        settle(nrm, fin_send.at[0])
        settle(fin_s, fin_send.at[1])
        settle(col_r.at[last], fin_send.at[2])
        for it in range(ITERS):
            settle(row_r.at[it, pl.ds(0, 15)], row_send.at[it])
            settle(col_r.at[it, pl.ds(0, 7)], col_send.at[it])

    @pl.when(on_one & (yh == 1))
    def _():
        for core in range(2):
            settle(tgt_f.at[core, rows56], take_send.at[core])
        settle(tmass, take_send.at[2])

    @pl.when(on_one & edge)
    def _():
        for far in range(1, 3):
            settle(src_f.at[0, rows56], swap_send.at[2 * far - 2])
            settle(smass.at[0], swap_send.at[2 * far - 1])


def finish(sum_ref, row_in, col_in, out_hbm, row_ref, col_ref, tile, sem):
    copies = []
    for n in range(8):
        rows = pl.ds(n * 64, 64)
        for j in range(4):
            lanes = pl.ds(j * 128, 128)
            tile[rows, lanes] = (sum_ref[rows, lanes] + col_in[pl.ds(j, 1), :]) * LN2
        copies.append(pltpu.make_async_copy(tile.at[rows], out_hbm.at[rows], sem.at[n]))
        copies[-1].start()
    row_ref[...] = row_in[...]
    col_ref[...] = col_in[...] * LN2
    for copy in copies:
        copy.wait()


def shards(coupling, src_pcs, tgt_pcs, src_mass, tgt_mass):
    total_rows = coupling.shape[0] * lax.axis_size("src")
    total_cols = coupling.shape[1] * lax.axis_size("tgt")
    dma = pltpu.SemaphoreType.DMA
    full, vec = jax.ShapeDtypeStruct((BLK, BLK), f32), jax.ShapeDtypeStruct((4, 128), f32)
    in_vmem, anywhere = pl.BlockSpec(memory_space=pltpu.VMEM), pl.BlockSpec(memory_space=pl.ANY)
    tile = lambda *lead: pltpu.VMEM((*lead, 8, 128), f32)
    gram = lambda *lead: pltpu.VMEM((*lead, 32, 128), f32)
    sums, row, col = pl.pallas_call(
        functools.partial(kernel, total_rows, total_cols),
        out_shape=(pltpu.VMEM((BLK, BLK), f32), pltpu.VMEM((4, 128), f32), pltpu.VMEM((4, 128), f32)),
        in_specs=[anywhere] * 5,
        out_specs=[in_vmem] * 3,
        scratch_shapes=[
            pltpu.VMEM((BLK, BLK), bf16),
            pltpu.VMEM((PCS, BLK), bf16),
            pltpu.VMEM((PCS, BLK), bf16),
            pltpu.VMEM((PAD, BLK), bf16),
            pltpu.VMEM((2 * PAD, BLK), bf16),
            pltpu.VMEM((2, PAD, BLK), f32),
            pltpu.VMEM((2, PAD, BLK), f32),
            pltpu.VMEM((2, PAD, BLK), f32),
            pltpu.VMEM((2, 4, 128), f32),
            pltpu.VMEM((2, 4, 128), f32),
            pltpu.VMEM((2, 4, 128), f32),
            pltpu.VMEM((TWO, 4 * PAD), bf16),
            pltpu.VMEM((TWO, 4 * PAD), bf16),
            pltpu.VMEM((PAD, TWO), bf16),
            pltpu.VMEM((2 * PAD, TWO), bf16),
            pltpu.VMEM((2 * PAD, TWO), bf16),
            pltpu.VMEM((TWO, TWO), f32),
            pltpu.VMEM((TWO, TWO), f32),
            pltpu.VMEM((TWO, 128), f32),
            tile(),
            gram(),
            gram(8),
            gram(),
            gram(8),
            gram(),
            gram(8),
            gram(),
            tile(ITERS),
            tile(ITERS, 16),
            tile(ITERS),
            tile(ITERS, 8),
            tile(),
            dma((5,)),
            dma((4,)),
            dma((4,)),
            dma((3,)),
            dma((3,)),
            dma((3,)),
            dma((3,)),
            dma((ITERS,)),
            dma((ITERS,)),
            dma((ITERS,)),
            dma((ITERS,)),
            dma((3,)),
            dma((3,)),
        ],
        compiler_params=pltpu.CompilerParams(collective_id=0, has_side_effects=True),
        name="coupling_step",
    )(coupling, src_pcs, tgt_pcs, src_mass.reshape(4, 128), tgt_mass.reshape(4, 128))
    out, row, col = pl.pallas_call(
        finish,
        out_shape=(full, vec, vec),
        in_specs=[in_vmem] * 3,
        out_specs=[anywhere, in_vmem, in_vmem],
        scratch_shapes=[pltpu.VMEM((BLK, BLK), f32), dma((8,))],
        compiler_params=pltpu.CompilerParams(vmem_limit_bytes=8 << 20),
        name="finish",
    )(*(pltpu.with_memory_space_constraint(v, pltpu.VMEM) for v in (sums, row, col)))
    return out, row.reshape(-1), col.reshape(-1)


def solution(mesh):
    in_specs = (P("src", "tgt"), P(None, "src"), P(None, "tgt"), P("src"), P("tgt"))
    out_specs = (P("src", "tgt"), P("src"), P("tgt"))
    return jax.shard_map(shards, mesh=mesh, in_specs=in_specs, out_specs=out_specs, check_vma=False)
```

```python
import functools
import math

import jax
import jax.numpy as jnp
from jax import lax
from jax.experimental import pallas as pl
from jax.experimental.pallas import tpu as pltpu
from jax.sharding import PartitionSpec as P

PCS = 50
ITERS = 4
eps_reg = 0.5
marg_power = 1.0 / (1.0 + eps_reg)
tiny_eps = 1e-06
LN2 = math.log(2.0)
LOG2E = 1.0 / LN2

PAD = 64
SENT = 56
HELD = 26
BLK = 512
TWO = 2 * BLK
MESH = pl.DeviceIdType.MESH
f32, bf16 = jnp.float32, jnp.bfloat16
FAR_X, FAR_8 = (2, 1, 3), (4, 3, 5, 2, 6, 1, 7)


def hops(d):
    return min(d[0], 4 - d[0]) + min(d[1], 8 - d[1])


NEAR = sorted(
    (
        min(((dx, dy), ((dx + 2) % 4, dy + 4)), key=lambda d: (hops(d), (d[0] + d[1]) % 2, d))
        for dx in range(4)
        for dy in range(4)
    ),
    key=hops,
    reverse=True,
)[:-1]


def coords():
    s, t = lax.axis_index("src"), lax.axis_index("tgt")
    return t // 8, (s % 2) * 4 + (t // 2) % 4, s // 2, t % 2


def device(x, y, z, c):
    return (z * 2 + y // 4, (x * 4 + y % 4) * 2 + c)


def split3(v):
    hi = v.astype(bf16)
    rest = v - hi.astype(f32)
    mid = rest.astype(bf16)
    lo = (rest - mid.astype(f32)).astype(bf16)
    return jnp.concatenate([hi, mid, lo], axis=0)


def fold3(v):
    n = v.shape[0] // 3
    return (v[:n] + v[n : 2 * n]) + v[2 * n :]


def thrice(v):
    return jnp.concatenate([v, v, v, jnp.zeros_like(v)], axis=0).T.astype(bf16)


def stack4(v):
    terms = split3(v)
    return jnp.concatenate([terms, jnp.zeros((PAD, v.shape[1]), bf16)], axis=0)


def turn(pot):
    return jnp.concatenate([pot, jnp.zeros((120, 128), f32)], axis=0).T


def join(top, total, v):
    high = jnp.maximum(top, jnp.max(v, axis=0))
    return high, total * jnp.exp2(top - high) + jnp.sum(jnp.exp2(v - high[None]), axis=0)


def over_rows(tops, sums):
    top = jnp.max(tops, axis=0, keepdims=True)
    return top + jnp.log2(jnp.sum(sums * jnp.exp2(tops - top), axis=0, keepdims=True))


def logsum_pass(table, pot, shift, out):
    turned = turn(pot)
    for pair in range(4):
        tops = [jnp.full((8, 128), -1e30, f32)] * 2
        sums = [jnp.zeros((8, 128), f32)] * 2
        for p in range(8):
            rows = pl.ds(p * 128, 128)
            if pair == 0:
                moved = jnp.broadcast_to(turned[:, p : p + 1], (128, 128))
                shift[rows, :] = moved
            else:
                moved = shift[rows, :]
            moved = moved.reshape(16, 8, 128)
            for k in range(2):
                j = 2 * pair + k
                v = table[rows, j * 128 : (j + 1) * 128].reshape(16, 8, 128) + moved
                tops[k], sums[k] = join(tops[k], sums[k], v)
        for k in range(2):
            out[pl.ds(2 * pair + k, 1), :] = over_rows(tops[k], sums[k])


def potentials(v, log_mass, log_count):
    top = jnp.max(v, axis=0)
    total = top + jnp.log2(jnp.sum(jnp.exp2(v - top[None]), axis=0))
    return marg_power * (log_mass - (total - log_count))


def send(src, dst, send_sem, recv_sem, target):
    pltpu.make_async_remote_copy(
        src_ref=src, dst_ref=dst, send_sem=send_sem, recv_sem=recv_sem,
        device_id=target, device_id_type=MESH,
    ).start()


def settle(ref, sem):
    pltpu.make_async_copy(ref, ref, sem).wait()


def greet(targets):
    barrier = pltpu.get_barrier_semaphore()
    for target in targets:
        pl.semaphore_signal(barrier, inc=1, device_id=target, device_id_type=MESH)


def kernel(
    total_rows, total_cols,
    coupling_hbm, src_hbm, tgt_hbm, smass_hbm, tmass_hbm,
    sum_ref, row_ref, col_ref,
    coupling, src_in, tgt_in, src_b, tgt_two, src_f, tgt_f, tgt_k, smass, tmass, tmass_k,
    src_t, tgt_t, src_all, tgt_all, tgt_own, scores, scores_t, shift, pot,
    m0_s, m0_r, m1_s, m1_r, m2_s, m2_r, nrm, row_s, row_r, col_s, col_r, fin_s,
    load_sem, swap_send, swap_recv, take_send, take_recv, m_send, m_recv, row_send, row_recv, col_send, col_recv, fin_send, fin_recv,
):
    x, y, z, c = coords()
    yh, yl = y // 4, y % 4
    on_one, on_zero = c == 1, c == 0

    loads = [
        pltpu.make_async_copy(src_hbm, src_in, load_sem.at[0]),
        pltpu.make_async_copy(tgt_hbm, tgt_in, load_sem.at[1]),
        pltpu.make_async_copy(coupling_hbm, coupling, load_sem.at[2]),
        pltpu.make_async_copy(smass_hbm, smass.at[yh], load_sem.at[3]),
        pltpu.make_async_copy(tmass_hbm, tmass.at[c], load_sem.at[4]),
    ]
    for copy in loads:
        copy.start()

    held = pl.ds(0, HELD)
    for ref in (m0_r, m1_r, m2_r):
        ref[:, pl.ds(HELD, 32 - HELD), :] = jnp.zeros((8, 32 - HELD, 128), f32)

    plane = sorted({*NEAR, *((dx, 0) for dx in FAR_X), *((0, dy) for dy in FAR_8)}, key=hops, reverse=True)
    ones = [device((x + dx) % 4, (y + dy) % 8, z, 1) for dx, dy in plane]
    ones += [device(x, y, (z + dz) % 8, 1) for dz in FAR_8]
    near = [device((x + dx) % 4, y, z, 0) for dx in (2, 1, 3, 0)]

    @pl.when(on_one)
    def _():
        greet(ones + near)

    @pl.when(on_zero)
    def _():
        greet([device(x, y, (z + dz) % 8, 1) for dz in FAR_8])
        greet([device((x + dx) % 4, y, z, 1) for dx in (2, 1, 3, 0)])

    src_b[...] = jnp.zeros((PAD, BLK), bf16)
    tgt_two[pl.ds(48, 16), :] = jnp.zeros((16, BLK), bf16)
    tgt_two[pl.ds(112, 16), :] = jnp.zeros((16, BLK), bf16)
    for copy in loads[:2]:
        copy.wait()
    src_b[pl.ds(0, HELD), :] = src_in[pl.ds(0, HELD), :]
    src_b[pl.ds(32, PCS - HELD), :] = src_in[pl.ds(HELD, PCS - HELD), :]
    tgt_two[pl.ds(0, PCS), :] = tgt_in[...]
    tgt_two[pl.ds(PAD, PCS), :] = tgt_in[...]
    loads[2].wait()

    panel = jnp.dot(src_b[...], coupling[...], preferred_element_type=f32)
    wide = fold3(
        lax.dot_general(
            split3(panel), tgt_two[...], (((1,), (1,)), ((), ())), preferred_element_type=f32
        )
    )
    left = lax.broadcasted_iota(jnp.int32, (32, 128), 1) < PAD
    packed = jnp.where(left, wide[:32], wide[32:])
    m0_s[...] = packed

    barrier = pltpu.get_barrier_semaphore()
    own0 = 2 * x + c

    @pl.when(on_one)
    def _():
        pl.semaphore_wait(barrier, len(ones) + 7 + 4)
        m0_r[own0, held] = packed[:HELD]
        for dx in FAR_X:
            send(m0_s.at[held], m0_r.at[own0, held], m_send.at[0], m_recv.at[0], device((x + dx) % 4, y, z, 1))

    @pl.when(on_zero)
    def _():
        pl.semaphore_wait(barrier, 4)
        for dx in (2, 1, 3, 0):
            send(m0_s.at[held], m0_r.at[own0, held], m_send.at[0], m_recv.at[0], device((x + dx) % 4, y, z, 1))

    for side in range(2):
        tgt_k[side, pl.ds(SENT, 8), :] = jnp.zeros((8, BLK), f32)
    for ref, own, block in ((src_f, yh, src_b), (tgt_f, c, tgt_two)):
        for side in range(2):
            ref[side, pl.ds(SENT, 8), :] = jnp.zeros((8, BLK), f32)
        ref[own, pl.ds(0, SENT), :] = block[pl.ds(0, PAD), :].astype(f32)[:SENT]
    for copy in loads[3:]:
        copy.wait()

    rows56 = pl.ds(0, SENT)

    def moment_of(packed_sum):
        return packed_sum * (total_rows * total_cols) ** (-0.5)

    def factor_of(packed_sum):
        moment = moment_of(packed_sum)
        square = jnp.sum(moment * moment, axis=0, keepdims=True)
        square = jnp.sum(square, axis=1, keepdims=True) * (1.0 / (PCS * PCS))
        return (2.0 / (eps_reg * PCS) * LOG2E) / jnp.sqrt(square + tiny_eps)

    def packed_two(v):
        return jnp.concatenate([jnp.where(left, v, 0.0), jnp.where(left, 0.0, v)], axis=0)

    log_rows, log_cols = math.log2(total_rows), math.log2(total_cols)
    partner = device(x, y, z, 1 - c)
    last = ITERS - 1

    @pl.when(on_zero)
    def _():
        send(tgt_f.at[0, rows56], tgt_f.at[0, rows56], swap_send.at[0], swap_recv.at[0], partner)
        send(tmass.at[0], tmass.at[0], swap_send.at[1], swap_recv.at[1], partner)
        src_t[pl.ds(0, BLK), :] = thrice(src_f[yh])
        log_tgt = jnp.log2(tmass[0])

        settle(nrm, fin_recv.at[0])
        two = packed_two(moment_of(nrm[...]))
        raw = fold3(jnp.dot(split3(two), tgt_two[...], preferred_element_type=f32))
        sum_ref[...] = jnp.dot(
            src_t[pl.ds(0, BLK), :], stack4(raw * factor_of(nrm[...])), preferred_element_type=f32
        )

        settle(pot, fin_recv.at[1])
        half = jnp.where(yh == 0, pot[pl.ds(0, 4), :], pot[pl.ds(4, 4), :])
        row_ref[...] = half * LN2
        turned = turn(jnp.concatenate([half, jnp.zeros((4, 128), f32)], axis=0))
        for p in range(4):
            rows = pl.ds(p * 128, 128)
            moved = jnp.broadcast_to(turned[:, p : p + 1], (128, 128))
            for j in range(4):
                lanes = pl.ds(j * 128, 128)
                sum_ref[rows, lanes] = sum_ref[rows, lanes] + moved

        settle(col_r.at[last], col_recv.at[last])
        col_ref[...] = potentials(col_r[last][:, :4, :], log_tgt, log_rows)

        settle(m0_r.at[pl.ds(0, 4), held], m_send.at[0])
        settle(tgt_f.at[0, rows56], swap_send.at[0])
        settle(tmass.at[0], swap_send.at[1])

    edge = (yl == 0) | (yl == 3)

    @pl.when(on_one & edge)
    def _():
        way = jnp.where(yl == 3, 1, 7)
        for far in range(1, 3):
            target = device(x, (y + far * way) % 8, z, 1)
            send(src_f.at[yh, rows56], src_f.at[yh, rows56], swap_send.at[2 * far - 2], swap_recv.at[2], target)
            send(smass.at[yh], smass.at[yh], swap_send.at[2 * far - 1], swap_recv.at[3], target)

    @pl.when(on_one)
    def _():
        settle(m0_r.at[pl.ds(0, 7), held], m_recv.at[0])
        part = jnp.sum(m0_r[...], axis=0)
        m1_s[...] = part
        for dy in FAR_8:
            send(m1_s.at[held], m1_r.at[y, held], m_send.at[1], m_recv.at[1], device(x, (y + dy) % 8, z, 1))
        m1_r[y, held] = part[:HELD]

        settle(tgt_f.at[0, rows56], swap_recv.at[0])
        settle(tmass.at[0], swap_recv.at[1])

        @pl.when(yh == 1)
        def _():
            target = device((x + 2) % 4, y, z, 1)
            for core in range(2):
                send(tgt_f.at[core, rows56], tgt_k.at[core, rows56], take_send.at[core], take_recv.at[core], target)
            send(tmass, tmass_k, take_send.at[2], take_recv.at[2], target)

        @pl.when(yh == 0)
        def _():
            for core in range(2):
                tgt_k[core, rows56, :] = tgt_f[core, rows56, :]
            tmass_k[...] = tmass[...]

        for core in range(2):
            lanes = pl.ds(core * BLK, BLK)
            block = tgt_f[core].astype(bf16)
            tgt_own[pl.ds(0, PAD), lanes] = block
            tgt_own[pl.ds(PAD, PAD), lanes] = block

        settle(m1_r.at[pl.ds(0, 7), held], m_recv.at[1])
        part = jnp.sum(m1_r[...], axis=0)
        m2_s[...] = part
        for dz in FAR_8:
            send(m2_s.at[held], m2_r.at[z, held], m_send.at[2], m_recv.at[2], device(x, y, (z + dz) % 8, 1))
        m2_r[z, held] = part[:HELD]

        settle(src_f.at[0, rows56], swap_recv.at[2])
        settle(smass.at[0], swap_recv.at[3])
        for side in range(2):
            src_t[pl.ds(side * BLK, BLK), :] = thrice(src_f[side])
            src_all[:, pl.ds(side * BLK, BLK)] = src_f[side].astype(bf16)
        log_src = jnp.log2(jnp.concatenate([smass[0], smass[1]], axis=0))
        log_own = jnp.log2(jnp.concatenate([tmass[0], tmass[1]], axis=0))

        @pl.when(yh == 1)
        def _():
            for core in range(2):
                settle(tgt_k.at[core, rows56], take_recv.at[core])
            settle(tmass_k, take_recv.at[2])

        log_tgt = jnp.log2(jnp.concatenate([tmass_k[0], tmass_k[1]], axis=0))
        for core in range(2):
            lanes = pl.ds(core * BLK, BLK)
            tgt_t[lanes, :] = thrice(tgt_k[core])
            block = tgt_k[core].astype(bf16)
            tgt_all[pl.ds(0, PAD), lanes] = block
            tgt_all[pl.ds(PAD, PAD), lanes] = block

        settle(m2_r.at[pl.ds(0, 7), held], m_recv.at[2])
        total = jnp.sum(m2_r[...], axis=0)
        nrm[...] = total
        send(nrm, nrm, fin_send.at[0], fin_recv.at[0], partner)

        turned = jnp.concatenate([packed_two(moment_of(total)), jnp.zeros((PAD, 128), f32)], axis=0).T
        back = turned[:PAD, :PAD] + turned[PAD:, :PAD]
        factor = factor_of(total)
        raw = fold3(jnp.dot(split3(back), src_all[...], preferred_element_type=f32))
        weighted_t = stack4(raw * factor)
        tops = [jnp.full((8, 128), -1e30, f32)] * 8
        sums = [jnp.zeros((8, 128), f32)] * 8
        for n in range(9):
            if n < 8:
                rows = pl.ds(n * 128, 128)
                scores_t[rows, :] = jnp.dot(tgt_t[rows, :], weighted_t, preferred_element_type=f32)
            if n:
                rows = pl.ds((n - 1) * 128, 128)
                for j in range(8):
                    v = scores_t[rows, j * 128 : (j + 1) * 128].reshape(16, 8, 128)
                    tops[j], sums[j] = join(tops[j], sums[j], v)
        for j in range(8):
            row_s[0, pl.ds(j, 1), :] = over_rows(tops[j], sums[j])

        row_slot = 4 * ((x + 2 * yh) % 4) + yl

        def score(targets):
            two = packed_two(moment_of(nrm[...]))
            raw = fold3(jnp.dot(split3(two), targets[...], preferred_element_type=f32))
            weighted = stack4(raw * factor_of(nrm[...]))
            for n in range(8):
                rows = pl.ds(n * 128, 128)
                scores[rows, :] = jnp.dot(src_t[rows, :], weighted, preferred_element_type=f32)

        def iteration(it, _):
            for dx, dy in NEAR:
                target = device((x + 4 - dx) % 4, (y + 8 - dy) % 8, z, 1)
                send(row_s.at[it], row_r.at[it, row_slot], row_send.at[it], row_recv.at[it], target)
            row_r[it, row_slot] = row_s[it]

            @pl.when(it == 0)
            def _():
                score(tgt_all)

            @pl.when(it == last)
            def _():
                score(tgt_own)

            settle(row_r.at[it, pl.ds(0, 15)], row_recv.at[it])
            row_pot = potentials(row_r[it], log_src, log_cols)
            pot[...] = row_pot

            @pl.when(it == last)
            def _():
                fin_s[...] = row_pot
                send(fin_s, pot, fin_send.at[1], fin_recv.at[1], partner)

            logsum_pass(scores, row_pot, shift, col_s.at[it])
            for dz in FAR_8:
                send(col_s.at[it], col_r.at[it, z], col_send.at[it], col_recv.at[it], device(x, y, (z + dz) % 8, 1))
            col_r[it, z] = col_s[it]

            @pl.when(it == last)
            def _():
                for dz in (*FAR_8, 0):
                    target = device(x, y, (z + dz) % 8, 0)
                    send(col_s.at[it], col_r.at[it, z], fin_send.at[2], col_recv.at[it], target)
                row_ref[...] = jnp.where(yh == 0, row_pot[:4], row_pot[4:]) * LN2
                for n in range(4):
                    to = pl.ds(n * 128, 128)
                    rows = pl.ds(pl.multiple_of(yh * BLK + n * 128, 128), 128)
                    moved = shift[rows, :]
                    for j in range(4):
                        sum_ref[to, pl.ds(j * 128, 128)] = scores[rows, pl.ds(BLK + j * 128, 128)] + moved

            settle(col_r.at[it, pl.ds(0, 7)], col_recv.at[it])
            pot[...] = potentials(col_r[it], jnp.where(it == last, log_own, log_tgt), log_rows)

            @pl.when(it < last)
            def _():
                logsum_pass(scores_t, pot[...], shift, row_s.at[it + 1])

            return 0

        lax.fori_loop(0, ITERS, iteration, 0)
        col_ref[...] = pot[pl.ds(4, 4), :]

        settle(m0_r.at[pl.ds(0, 3), held], m_send.at[0])
        settle(m1_r.at[pl.ds(0, 7), held], m_send.at[1])
        settle(m2_r.at[pl.ds(0, 7), held], m_send.at[2])
        settle(nrm, fin_send.at[0])
        settle(fin_s, fin_send.at[1])
        settle(col_r.at[last], fin_send.at[2])
        for it in range(ITERS):
            settle(row_r.at[it, pl.ds(0, 15)], row_send.at[it])
            settle(col_r.at[it, pl.ds(0, 7)], col_send.at[it])

    @pl.when(on_one & (yh == 1))
    def _():
        for core in range(2):
            settle(tgt_f.at[core, rows56], take_send.at[core])
        settle(tmass, take_send.at[2])

    @pl.when(on_one & edge)
    def _():
        for far in range(1, 3):
            settle(src_f.at[0, rows56], swap_send.at[2 * far - 2])
            settle(smass.at[0], swap_send.at[2 * far - 1])


def finish(sum_ref, row_in, col_in, out_hbm, row_ref, col_ref, tile, sem):
    copies = []
    for n in range(8):
        rows = pl.ds(n * 64, 64)
        for j in range(4):
            lanes = pl.ds(j * 128, 128)
            tile[rows, lanes] = (sum_ref[rows, lanes] + col_in[pl.ds(j, 1), :]) * LN2
        copies.append(pltpu.make_async_copy(tile.at[rows], out_hbm.at[rows], sem.at[n]))
        copies[-1].start()
    row_ref[...] = row_in[...]
    col_ref[...] = col_in[...] * LN2
    for copy in copies:
        copy.wait()


def shards(coupling, src_pcs, tgt_pcs, src_mass, tgt_mass):
    total_rows = coupling.shape[0] * lax.axis_size("src")
    total_cols = coupling.shape[1] * lax.axis_size("tgt")
    dma = pltpu.SemaphoreType.DMA
    full, vec = jax.ShapeDtypeStruct((BLK, BLK), f32), jax.ShapeDtypeStruct((4, 128), f32)
    in_vmem, anywhere = pl.BlockSpec(memory_space=pltpu.VMEM), pl.BlockSpec(memory_space=pl.ANY)
    tile = lambda *lead: pltpu.VMEM((*lead, 8, 128), f32)
    gram = lambda *lead: pltpu.VMEM((*lead, 32, 128), f32)
    sums, row, col = pl.pallas_call(
        functools.partial(kernel, total_rows, total_cols),
        out_shape=(pltpu.VMEM((BLK, BLK), f32), pltpu.VMEM((4, 128), f32), pltpu.VMEM((4, 128), f32)),
        in_specs=[anywhere] * 5,
        out_specs=[in_vmem] * 3,
        scratch_shapes=[
            pltpu.VMEM((BLK, BLK), bf16),
            pltpu.VMEM((PCS, BLK), bf16),
            pltpu.VMEM((PCS, BLK), bf16),
            pltpu.VMEM((PAD, BLK), bf16),
            pltpu.VMEM((2 * PAD, BLK), bf16),
            pltpu.VMEM((2, PAD, BLK), f32),
            pltpu.VMEM((2, PAD, BLK), f32),
            pltpu.VMEM((2, PAD, BLK), f32),
            pltpu.VMEM((2, 4, 128), f32),
            pltpu.VMEM((2, 4, 128), f32),
            pltpu.VMEM((2, 4, 128), f32),
            pltpu.VMEM((TWO, 4 * PAD), bf16),
            pltpu.VMEM((TWO, 4 * PAD), bf16),
            pltpu.VMEM((PAD, TWO), bf16),
            pltpu.VMEM((2 * PAD, TWO), bf16),
            pltpu.VMEM((2 * PAD, TWO), bf16),
            pltpu.VMEM((TWO, TWO), f32),
            pltpu.VMEM((TWO, TWO), f32),
            pltpu.VMEM((TWO, 128), f32),
            tile(),
            gram(),
            gram(8),
            gram(),
            gram(8),
            gram(),
            gram(8),
            gram(),
            tile(ITERS),
            tile(ITERS, 16),
            tile(ITERS),
            tile(ITERS, 8),
            tile(),
            dma((5,)),
            dma((4,)),
            dma((4,)),
            dma((3,)),
            dma((3,)),
            dma((3,)),
            dma((3,)),
            dma((ITERS,)),
            dma((ITERS,)),
            dma((ITERS,)),
            dma((ITERS,)),
            dma((3,)),
            dma((3,)),
        ],
        compiler_params=pltpu.CompilerParams(collective_id=0, has_side_effects=True),
        name="coupling_step",
    )(coupling, src_pcs, tgt_pcs, src_mass.reshape(4, 128), tgt_mass.reshape(4, 128))
    out, row, col = pl.pallas_call(
        finish,
        out_shape=(full, vec, vec),
        in_specs=[in_vmem] * 3,
        out_specs=[anywhere, in_vmem, in_vmem],
        scratch_shapes=[pltpu.VMEM((BLK, BLK), f32), dma((8,))],
        compiler_params=pltpu.CompilerParams(vmem_limit_bytes=8 << 20),
        name="finish",
    )(*(pltpu.with_memory_space_constraint(v, pltpu.VMEM) for v in (sums, row, col)))
    return out, row.reshape(-1), col.reshape(-1)


def solution(mesh):
    in_specs = (P("src", "tgt"), P(None, "src"), P(None, "tgt"), P("src"), P("tgt"))
    out_specs = (P("src", "tgt"), P("src"), P("tgt"))
    return jax.shard_map(shards, mesh=mesh, in_specs=in_specs, out_specs=out_specs, check_vma=False)
```
